512 devices in a mesh: stream: 32 (over z, core), girth: 16 (over y, x).
Axes of the slice: x: 4, y: 4, z: 16, core: 2. Of those that a mesh axis runs over, the one named last changes fastest.
Arguments:
- state: float32 [64, 7, 128, 128], P('stream', None, 'girth'), may hold values from -1.8 to 1.8
- propeller: float32 [7, 131072], P(None, ('stream', 'girth')), may hold values from -6 to 6
- donor_index: int32 [512, 128], P(('stream', 'girth')), may hold values from -1 to 255, as said below
- fringe_index: int32 [512, 128], P(('stream', 'girth')), may hold values from -1 to 2047, as said below
- donor_weight: float32 [512, 128], P(('stream', 'girth')), may hold values from 0.25 to 1
- disk_mask: int32 [64, 128, 128], P('stream', 'girth'), may hold values 0 or 1
- thrust: float32 [7], replicated, may hold values from -1.8 to 1.8
- face: float32 [64, 6, 128, 128], P('stream', None, 'girth'), may hold values from 0.2 to 1
- coupling: float32 [6, 7, 7], replicated, may hold values from -0.875 to 0.875
- diag_inverse: bfloat16 [64, 7, 7, 128, 128], P('stream', None, None, 'girth'), may hold values from -0.15039062 to 1
- lower_jacobian: float32 [7, 7], replicated, may hold values from -0.06 to 1.06
- upper_jacobian: float32 [7, 7], replicated, may hold values from -0.06 to 1.06
Outputs:
- new_state: float32 [64, 7, 128, 128], P('stream', None, 'girth')
- residual: float32 [64, 7, 128, 128], P('stream', None, 'girth')
The draws below stay inside these ranges and needn't reach their ends.
Inputs may be any that keep to these rules, and one draw needn't show every extreme that they name: `donor_index`: live slots of one device and peer come first; every device of one streamwise index fills all 8 slots toward one common peer. `fringe_index`: equal to -1 exactly where donor_index is -1.
All inputs are finite; a program needn't handle non-finite values. No bound on the sum of `disk_mask` on one device may be relied on, other than what follows from the above.
Results may differ from the reference program's by a relative error of at most 0.0003.
Values sent between devices are 32-bit elements; how exact they have to be, the bound alone decides.
No kernel may reach another device: no remote copies, remote signals or barrier semaphores. Data moves between devices by JAX's collectives and lax.ppermute only.
A program may use at most 64 MiB of HBM per device.

```python
import math
import jax
import jax.numpy as jnp
from jax import lax

VARS = 7
CS = 2
CG = 8
CN = 128
PROP_DEV = 256
CAP = 8
STREAM_CELLS = 64
NG = 128
SENDERS = 512
PROP = 131072
N_STREAM = 32
N_GIRTH = 16


def overset_layout(key):
    base = jax.random.fold_in(key, 17)
    entry_counts = jax.random.randint(jax.random.fold_in(base, 1), (N_STREAM, N_GIRTH, N_GIRTH), 1, CAP + 1)
    busy_peer = jax.random.randint(jax.random.fold_in(base, 2), (N_STREAM, 1, 1), 0, N_GIRTH)
    peer_index = jnp.arange(N_GIRTH)[None, None, :]
    sender_index = jnp.arange(N_GIRTH)[None, :, None]
    entry_counts = jnp.where(peer_index == busy_peer, CAP, entry_counts)
    quiet_peer = (busy_peer + 1) % N_GIRTH
    entry_counts = jnp.where((sender_index == 0) & (peer_index == quiet_peer), 1, entry_counts)
    position_index = jnp.arange(CAP)[None, None, None, :]
    is_live = position_index < entry_counts[..., None]
    marked = ((sender_index == 0) & (peer_index == busy_peer))[..., None]
    return (is_live, marked, position_index)


def draw_donor_index(key, part):
    is_live, marked, position_index = overset_layout(key)
    chosen = jax.random.randint(jax.random.fold_in(key, 21), is_live.shape, 0, PROP_DEV)
    chosen = jnp.where(marked & (position_index == 0), PROP_DEV - 1, chosen)
    chosen = jnp.where(marked & (position_index == 1), 0, chosen)
    result = jnp.where(is_live, chosen, -1)
    return result.reshape(N_STREAM * N_GIRTH, N_GIRTH * CAP).astype(jnp.int32)


def draw_fringe_index(key, part):
    is_live, marked, position_index = overset_layout(key)
    chosen = jax.random.randint(jax.random.fold_in(key, 23), is_live.shape, 0, CS * CG * CN)
    chosen = jnp.where(marked & (position_index == 0), CS * CG * CN - 1, chosen)
    chosen = jnp.where(marked & (position_index == 1), 0, chosen)
    result = jnp.where(is_live, chosen, -1)
    return result.reshape(N_STREAM * N_GIRTH, N_GIRTH * CAP).astype(jnp.int32)


def draw_diag_inverse(key, part):
    full_shape = (STREAM_CELLS, 7, 7, NG, CN)
    first_key = jax.random.fold_in(key, 31)
    second_key = jax.random.fold_in(key, 32)
    tertiary_key = jax.random.fold_in(key, 33)
    diagonal = jax.random.uniform(first_key, (STREAM_CELLS, 7, 1, NG, CN), jnp.float32, 0.9, 1.0)
    off_diagonal = jnp.clip(0.035 * jax.random.normal(second_key, full_shape, jnp.float32), -0.15, 0.15)
    packet_groups = jax.random.randint(tertiary_key, (3,), 0, STREAM_CELLS)
    packet_rows = jnp.any(jnp.arange(STREAM_CELLS)[:, None] == packet_groups[None, :], axis=1)
    scale_factor = jnp.where(packet_rows, 0.6, 1.0).astype(jnp.float32)[:, None, None, None, None]
    unit = jnp.eye(7, dtype=jnp.float32)[None, :, :, None, None]
    return (unit * diagonal * scale_factor + (1.0 - unit) * off_diagonal).astype(jnp.bfloat16)


def draw_lower_jacobian(key, part):
    first_key = jax.random.fold_in(key, 41)
    second_key = jax.random.fold_in(key, 42)
    ranking = jax.random.permutation(first_key, 7)
    slow_channel = ranking < 4
    rates = jnp.where(slow_channel, jnp.exp(-2.3 / STREAM_CELLS), jnp.exp(-1.0 / 40.0)).astype(jnp.float32)
    off_diagonal = jnp.clip(0.015 * jax.random.normal(second_key, (7, 7), jnp.float32), -0.06, 0.06)
    unit = jnp.eye(7, dtype=jnp.float32)
    return unit * (rates / 0.95)[:, None] + (1.0 - unit) * off_diagonal


def draw_upper_jacobian(key, part):
    first_key = jax.random.fold_in(key, 51)
    second_key = jax.random.fold_in(key, 52)
    ranking = jax.random.permutation(first_key, 7)
    slow_channel = ranking < 4
    rates = jnp.where(slow_channel, jnp.exp(-2.3 / STREAM_CELLS), jnp.exp(-1.0 / 32.0)).astype(jnp.float32)
    off_diagonal = jnp.clip(0.015 * jax.random.normal(second_key, (7, 7), jnp.float32), -0.06, 0.06)
    unit = jnp.eye(7, dtype=jnp.float32)
    return unit * (rates / 0.95)[:, None] + (1.0 - unit) * off_diagonal


def plant(array, rng, least, high):
    longest = array.shape.index(max(array.shape))
    spots = []
    for shift in (0, 1):
        where = [jax.random.randint(jax.random.fold_in(rng, axis), (), 0, length) for axis, length in enumerate(array.shape)]
        where[longest] = (where[longest] + shift) % array.shape[longest]
        spots.append(tuple(where))
    return array.at[spots[0]].set(least).at[spots[1]].set(high)


def level_of(rng, extent, cuts, least, high):
    level, own = 1.0, jax.random.fold_in(rng, 6)
    for dim, blocks in cuts:
        steps = jnp.exp(jax.random.uniform(jax.random.fold_in(own, dim), (blocks,), jnp.float32, least / len(cuts), high / len(cuts)))
        level = level * jnp.repeat(steps, extent[dim] // blocks).reshape([-1 if axis == dim else 1 for axis in range(len(extent))])
    return level


def gaussian(own_key, extent, width, limit, split=(), kind=jnp.bfloat16):
    array = jax.random.normal(own_key, extent, jnp.float32) * width
    if len(split) > 0:
        array = level_of(own_key, extent, split, -0.22, 0.18) * array
    return jnp.clip(array, min=-limit, max=limit).astype(kind)


def setup_inputs(seed: int = 0) -> dict:
    streams_of = jax.random.split(jax.random.key(seed), 13)
    state = gaussian(streams_of[0], (STREAM_CELLS, VARS, NG, CN), 0.3, 1.8, ((0, 32), (2, 16)), jnp.float32)
    propeller = gaussian(streams_of[1], (VARS, PROP), 1.0, 6.0, ((1, 512),), jnp.float32)
    donor_index = draw_donor_index(jax.random.fold_in(streams_of[12], 71), 0)
    fringe_index = draw_fringe_index(jax.random.fold_in(streams_of[12], 71), 0)
    donor_weight = jnp.clip(0.25 + 0.75 * jax.random.uniform(streams_of[4], (SENDERS, N_GIRTH * CAP), jnp.float32) ** level_of(streams_of[4], (SENDERS, N_GIRTH * CAP), ((0, 512),), -0.2, 0.2), 0.25, 1.0)
    disk_mask = plant((jax.random.randint(streams_of[5], (STREAM_CELLS, NG, CN), 0, 6) < 1).astype(jnp.int32), jax.random.fold_in(streams_of[5], 1), 0, 1)
    thrust = gaussian(streams_of[6], (VARS,), 0.3, 1.8, (), jnp.float32)
    face = jnp.clip(jnp.exp(math.log(1.0) - 1.609438 * jax.random.uniform(streams_of[7], (STREAM_CELLS, 6, NG, CN), jnp.float32) ** level_of(streams_of[7], (STREAM_CELLS, 6, NG, CN), ((0, 32), (2, 16)), -0.2, 0.2)), 0.2, 1.0)
    coupling = gaussian(streams_of[8], (6, VARS, VARS), 49 ** -0.5, 0.875, (), jnp.float32)
    diag_inverse = draw_diag_inverse(jax.random.fold_in(streams_of[12], 71), 0)
    lower_jacobian = draw_lower_jacobian(jax.random.fold_in(streams_of[12], 71), 0)
    upper_jacobian = draw_upper_jacobian(jax.random.fold_in(streams_of[12], 71), 0)
    return dict(state=state, propeller=propeller, donor_index=donor_index, fringe_index=fringe_index, donor_weight=donor_weight, disk_mask=disk_mask, thrust=thrust, face=face, coupling=coupling, diag_inverse=diag_inverse, lower_jacobian=lower_jacobian, upper_jacobian=upper_jacobian)


PRECISE = lax.Precision.HIGHEST


def residual_from(current, stream_pad, beside_all, face, coupling, disk_mask, thrust):
    normal_pad = jnp.pad(current, ((0, 0), (0, 0), (0, 0), (1, 1)))
    beside = [stream_pad[:-2], stream_pad[2:], beside_all[:, :, :-2], beside_all[:, :, 2:], normal_pad[..., :-2], normal_pad[..., 2:]]
    residual = disk_mask.astype(jnp.float32)[:, None] * thrust[None, :, None, None]
    for direction in range(6):
        residual = residual + face[:, direction:direction + 1] * jnp.einsum("ij,ajbc->aibc", coupling[direction], beside[direction] - current, precision=PRECISE)
    return residual


def forward_step(matrix):
    def advance(previous, inputs):
        inverse, source = inputs
        inverse = inverse.astype(jnp.float32)
        result = jnp.einsum("ijc,jc->ic", inverse, source + jnp.dot(matrix, previous, precision=PRECISE), precision=PRECISE)
        return result, result
    return advance


def backward_step(matrix):
    def advance(following, inputs):
        inverse, star = inputs
        inverse = inverse.astype(jnp.float32)
        result = star + jnp.einsum("ijc,jc->ic", inverse, jnp.dot(matrix, following, precision=PRECISE), precision=PRECISE)
        return result, result
    return advance


def reference(state, propeller, donor_index, fringe_index, donor_weight, disk_mask, thrust, face, coupling, diag_inverse, lower_jacobian, upper_jacobian):
    all_cells = STREAM_CELLS * NG * CN
    sender_ids = jnp.arange(N_STREAM * N_GIRTH, dtype=jnp.int32)[:, None]
    is_live = donor_index >= 0
    source_cols = (sender_ids * PROP_DEV + jnp.maximum(donor_index, 0)).astype(jnp.int32).reshape(-1)
    outgoing = jnp.take(propeller, source_cols, axis=1) * jnp.where(is_live, donor_weight, 0.0).reshape(-1)[None, :]
    slab_index = sender_ids // N_GIRTH
    peer_index = jnp.arange(N_GIRTH * CAP, dtype=jnp.int32)[None, :] // CAP
    target = jnp.maximum(fringe_index, 0)
    row_index = slab_index * CS + target // (CG * CN)
    girth_index = peer_index * CG + (target % (CG * CN)) // CN
    normal_index = target % CN
    flat_index = (row_index * NG + girth_index) * CN + normal_index
    flat_index = jnp.where(is_live, flat_index, all_cells).astype(jnp.int32).reshape(-1)
    accumulated = jnp.zeros((all_cells, 7), jnp.float32).at[flat_index].add(outgoing.T, mode="drop")
    hit_count = jnp.zeros((all_cells,), jnp.int32).at[flat_index].add(1, mode="drop")
    fringe = (hit_count > 0).reshape(STREAM_CELLS, 1, NG, CN)
    donated = accumulated.reshape(STREAM_CELLS, NG, CN, 7).transpose(0, 3, 1, 2)
    current = jnp.where(fringe, donated, state)
    stream_pad = jnp.pad(current, ((1, 1), (0, 0), (0, 0), (0, 0)))
    beside_all = jnp.concatenate([current[:, :, -1:], current, current[:, :, :1]], axis=2)
    residual = residual_from(current, stream_pad, beside_all, face, coupling, disk_mask, thrust)
    source = jnp.where(fringe, 0.0, -residual).reshape(STREAM_CELLS, 7, NG * CN)
    inverse = diag_inverse.reshape(STREAM_CELLS, 7, 7, NG * CN)
    start = jnp.zeros((7, NG * CN), jnp.float32)
    _, stars = lax.scan(forward_step(lower_jacobian), start, (inverse, source))
    _, updates = lax.scan(backward_step(upper_jacobian), start, (inverse, stars), reverse=True)
    new_state = current + updates.reshape(STREAM_CELLS, 7, NG, CN)
    return new_state, residual
```

```python
import jax
import jax.numpy as jnp
from jax import lax
from jax.experimental import pallas as pl
from jax.experimental.pallas import tpu as pltpu
from jax.sharding import PartitionSpec as P

F32 = jnp.float32
BF16 = jnp.bfloat16
VARS = 7
STREAMS = 32
GIRTHS = 16
DONOR_ROWS = 24
SEND_ROWS = 33
BACK_ROWS = 7
FLOW_VALUES = 32


def lanes(shape=(8, 128)):
    return lax.broadcasted_iota(jnp.int32, shape, len(shape) - 1)


def sublanes(shape=(8, 128)):
    return lax.broadcasted_iota(jnp.int32, shape, len(shape) - 2)


def split_parts(x):
    high = x.astype(BF16).astype(F32)
    rest = x - high
    middle = rest.astype(BF16).astype(F32)
    return high, middle, rest - middle


def block_transpose(a, b, c, d):
    lane = lanes()
    half = lane < 64
    even = (lane & 32) == 0
    a, c = jnp.where(half, a, pltpu.roll(c, 64, 1)), jnp.where(half, pltpu.roll(a, 64, 1), c)
    b, d = jnp.where(half, b, pltpu.roll(d, 64, 1)), jnp.where(half, pltpu.roll(b, 64, 1), d)
    a, b = jnp.where(even, a, pltpu.roll(b, 32, 1)), jnp.where(even, pltpu.roll(a, 96, 1), b)
    c, d = jnp.where(even, c, pltpu.roll(d, 32, 1)), jnp.where(even, pltpu.roll(c, 96, 1), d)
    return a, b, c, d


def donor_kernel(prop_ref, index_ref, fringe_ref, weight_ref, state_ref, out_ref):
    place = lax.axis_index("girth")
    index = index_ref[...]
    cells = lax.broadcasted_iota(jnp.int32, (256, 128), 0)
    pick = jnp.where(cells == index, 1.0, 0.0).astype(BF16)
    values = jnp.zeros((VARS, 128), F32)
    for part in split_parts(prop_ref[...]):
        values = values + jnp.dot(part.astype(BF16), pick, preferred_element_type=F32)
    values = values * weight_ref[...]
    target = jnp.where(index >= 0, fringe_ref[...], -1).astype(F32)
    edges = [
        (
            state_ref[pl.ds(row * 56, VARS, stride=8), :],
            state_ref[pl.ds(row * 56 + 7, VARS, stride=8), :],
        )
        for row in range(2)
    ]
    upper = lax.rem(place + 1, GIRTHS)
    for peer in range(GIRTHS):
        start = peer * DONOR_ROWS
        out_ref[start : start + VARS, :] = values
        out_ref[start + VARS : start + 8, :] = target
        out_ref[start + 8 : start + 24, :] = jnp.zeros((16, 128), F32)
        for row, (first, last) in enumerate(edges):
            at = start + 8 + row * 8
            out_ref[at : at + VARS, :] = jnp.where(upper == peer, last, first)


def fringe_sums(landed_ref, place):
    sub, lane = sublanes(), lanes()
    row = lanes((1, 128))
    slot = row & 31
    left = {}
    right = []
    for group in range(4):
        entries = jnp.zeros((8, 128), F32)
        for quarter in range(4):
            sender = group * 4 + quarter
            shift = lax.rem(32 * quarter + 8 - 8 * place + 128, 128)
            rolled = pltpu.roll(landed_ref[sender * DONOR_ROWS : sender * DONOR_ROWS + 8, :], shift, 1)
            entries = jnp.where((lane >> 5) == quarter, rolled, entries)
        target = entries[7:8, :].astype(jnp.int32)
        live = target >= 0
        tall = target >> 7
        own = jnp.where(live & (slot >= 8) & (slot < 16), tall, -1)
        low = jnp.where(live & (slot < 8) & ((tall & 7) == 7), tall >> 3, -1)
        high = jnp.where(live & (slot >= 16) & (slot < 24) & ((tall & 7) == 0), tall >> 3, -1)
        onto = lax.broadcasted_iota(jnp.int32, (128, 128), 0)
        right.append(jnp.where(onto == (target & 127), 1.0, 0.0).astype(BF16))
        parts = split_parts(entries)
        for which, part in enumerate(parts):
            counted = 1.0 if which == 0 else 0.0
            marked = jnp.where(sub == 7, counted, part)
            rows = []
            for r in range(2):
                inside = own == sub + 8 * r
                for v in range(8):
                    rows.append(jnp.where(inside, marked[v : v + 1, :], 0.0))
            for side in (low, high):
                for r in range(2):
                    rows.append(jnp.where(side == r, marked, 0.0))
            left[which, group] = jnp.concatenate(rows, axis=0).astype(BF16)
    right = jnp.concatenate(right, axis=1)
    total = None
    for which in range(3):
        lhs = jnp.concatenate([left[which, group] for group in range(4)], axis=1)
        part = lax.dot_general(lhs, right, (((1,), (1,)), ((), ())), preferred_element_type=F32)
        total = part if total is None else total + part
    return total


def flow_kernel(
    landed_ref,
    state_ref,
    face_ref,
    disk_ref,
    diag_ref,
    thrust_ref,
    coupling_ref,
    send_ref,
    current_ref,
):
    place = lax.axis_index("girth")
    sub, lane = sublanes(), lanes()
    sums = fringe_sums(landed_ref, place)
    edges = []
    for side, peer in enumerate((lax.rem(place + 15, GIRTHS), lax.rem(place + 1, GIRTHS))):
        both = []
        for r in range(2):
            start = pl.multiple_of(peer * DONOR_ROWS + 8 + 8 * r, 8)
            edge = landed_ref[pl.ds(start, 8), :]
            found = sums[128 + side * 16 + r * 8 : 136 + side * 16 + r * 8, :]
            both.append(jnp.where(found[7:8, :] > 0.5, found, edge))
        edges.append(both)
    current, fringe = [], []
    for r in range(2):
        block = sums[r * 64 : (r + 1) * 64, :]
        hit = block[56:64, :] > 0.5
        fringe.append(hit)
        current.append(
            [jnp.where(hit, block[v * 8 : v * 8 + 8, :], state_ref[r, v]) for v in range(VARS)]
        )
    zero = jnp.zeros((8, 128), F32)
    residual = []
    for r in range(2):
        own = current[r]
        disk = disk_ref[r].astype(F32)
        total = [disk * thrust_ref[i] for i in range(VARS)]
        for direction in range(6):
            if direction == 0:
                beside = current[0] if r == 1 else [zero] * VARS
            elif direction == 1:
                beside = current[1] if r == 0 else [zero] * VARS
            elif direction == 2:
                beside = [
                    jnp.where(sub == 0, edges[0][r][v : v + 1, :], pltpu.roll(own[v], 1, 0))
                    for v in range(VARS)
                ]
            elif direction == 3:
                beside = [
                    jnp.where(sub == 7, edges[1][r][v : v + 1, :], pltpu.roll(own[v], 7, 0))
                    for v in range(VARS)
                ]
            elif direction == 4:
                beside = [jnp.where(lane == 0, 0.0, pltpu.roll(own[v], 1, 1)) for v in range(VARS)]
            else:
                beside = [
                    jnp.where(lane == 127, 0.0, pltpu.roll(own[v], 127, 1)) for v in range(VARS)
                ]
            factor = face_ref[r, direction]
            jump = [factor * (beside[v] - own[v]) for v in range(VARS)]
            for i in range(VARS):
                for j in range(VARS):
                    total[i] = total[i] + coupling_ref[direction, i, j] * jump[j]
        residual.append(total)
        for v in range(VARS):
            current_ref[r, v] = own[v]

    def pack(k, four):
        for quarter, tile in enumerate(block_transpose(*four)):
            send_ref[pl.ds(quarter * 8 * SEND_ROWS + k, 8, stride=SEND_ROWS), :] = tile

    flow = residual[0] + residual[1] + current[0] + current[1]
    flow += [jnp.where(hit, 1.0, 0.0) for hit in fringe]
    flow += [face_ref[0, 0], face_ref[1, 1]]
    for k in range(FLOW_VALUES // 4):
        pack(k, flow[4 * k : 4 * k + 4])
    places = [(r, i, j) for r in range(2) for i in range(VARS) for j in range(VARS)]
    for k in range(25):
        four = [diag_ref[at].astype(F32) for at in places[4 * k : 4 * k + 4]]
        pack(FLOW_VALUES // 4 + k, four + [zero] * (4 - len(four)))


def from_before(x, count):
    sub, lane = sublanes(), lanes()
    if count == 4:
        return jnp.where(sub == 0, 0.0, pltpu.roll(x, 1, 0))
    width = 32 * count
    x = pltpu.roll(x, width, 1)
    return jnp.where(lane < width, jnp.where(sub == 0, 0.0, pltpu.roll(x, 1, 0)), x)


def from_after(x, count):
    sub, lane = sublanes(), lanes()
    if count == 4:
        return jnp.where(sub == 7, 0.0, pltpu.roll(x, 7, 0))
    width = 32 * count
    x = pltpu.roll(x, 128 - width, 1)
    return jnp.where(lane >= 128 - width, jnp.where(sub == 7, 0.0, pltpu.roll(x, 7, 0)), x)


def total_of(terms):
    while len(terms) > 1:
        terms = [sum(terms[at : at + 2]) for at in range(0, len(terms), 2)]
    return terms[0]


def apply(ref, vector, add=None):
    result = []
    for i in range(VARS):
        terms = [ref[i * VARS + j] * vector[j] for j in range(VARS)]
        result.append(total_of(terms + ([add[i]] if add is not None else [])))
    return result


def solve_kernel(
    moved_ref, coupling_ref, lower_ref, upper_ref, back_ref, diag, near, far, maps, moved_maps
):
    def unpack(k):
        return block_transpose(
            *[
                moved_ref[pl.ds(quarter * SEND_ROWS + k, 8, stride=4 * SEND_ROWS), :]
                for quarter in range(4)
            ]
        )

    flow = []
    for k in range(FLOW_VALUES // 4):
        flow += unpack(k)
    for k in range(25):
        for at, tile in enumerate(unpack(FLOW_VALUES // 4 + k)):
            if 4 * k + at < 98:
                diag[(4 * k + at) // 49, (4 * k + at) % 49] = tile
    residual = [flow[0:7], flow[7:14]]
    current = [flow[14:21], flow[21:28]]
    fringe = [flow[28] > 0.5, flow[29] > 0.5]
    factors = flow[30:32]
    beside = [
        [factors[0] * from_before(current[1][v], 1) for v in range(VARS)],
        [factors[1] * from_after(current[0][v], 1) for v in range(VARS)],
    ]
    for r in range(2):
        for i in range(VARS):
            for j in range(VARS):
                residual[r][i] = residual[r][i] + coupling_ref[r, i, j] * beside[r][j]
    source = [[jnp.where(fringe[r], 0.0, -residual[r][i]) for i in range(VARS)] for r in range(2)]

    def times(matrix_ref, out):
        for r in range(2):
            for i in range(VARS):
                row = [diag[r, i * VARS + j] for j in range(VARS)]
                for k in range(VARS):
                    out[r, i * VARS + k] = total_of(
                        [row[j] * matrix_ref[j, k] for j in range(VARS)]
                    )

    def multiply(a, b, out):
        for i in range(VARS):
            row = [a[i * VARS + j] for j in range(VARS)]
            for k in range(VARS):
                out[i * VARS + k] = total_of([row[j] * b[j * VARS + k] for j in range(VARS)])

    def scan(offset, shifted):
        for level, count in enumerate((1, 2)):
            a = maps.at[level]
            for at in range(49):
                moved_maps[at] = shifted(a[at], count)
            offset = apply(a, [shifted(x, count) for x in offset], offset)
            multiply(a, moved_maps, maps.at[level + 1])
        a = maps.at[2]
        x = offset
        for _ in range(7):
            x = apply(a, [shifted(part, 4) for part in x], offset)
        return x

    times(lower_ref, near)
    times(upper_ref, far)
    first = apply(diag.at[0], source[0])
    second = apply(near.at[1], first, apply(diag.at[1], source[1]))
    multiply(near.at[1], near.at[0], maps.at[0])
    second = scan(second, from_before)
    first = apply(near.at[0], [from_before(x, 1) for x in second], first)
    multiply(far.at[0], far.at[1], maps.at[0])
    update_first = scan(apply(far.at[0], second, first), from_after)
    update_second = apply(far.at[1], [from_after(x, 1) for x in update_first], second)

    results = update_first + update_second + residual[0] + residual[1]
    for k in range(BACK_ROWS):
        for quarter, tile in enumerate(block_transpose(*results[4 * k : 4 * k + 4])):
            back_ref[pl.ds(quarter * BACK_ROWS + k, 8, stride=4 * BACK_ROWS), :] = tile


def finish_kernel(returned_ref, current_ref, state_ref, residual_ref):
    results = []
    for k in range(BACK_ROWS):
        results += block_transpose(
            *[
                returned_ref[pl.ds(quarter * 8 * BACK_ROWS + k, 8, stride=BACK_ROWS), :]
                for quarter in range(4)
            ]
        )
    for r in range(2):
        for v in range(VARS):
            state_ref[r, v] = current_ref[r, v] + results[r * VARS + v]
            residual_ref[r, v] = results[14 + r * VARS + v]


VMEM = pl.BlockSpec(memory_space=pltpu.VMEM)
SMEM = pl.BlockSpec(memory_space=pltpu.SMEM)


def exchange(block, axis, parts):
    rows = block.shape[0] // parts
    if rows % 8 == 0:
        shaped = block.reshape(parts, rows, 128)
    else:
        shaped = block.reshape(block.shape[0], 1, 128)
    return lax.all_to_all(shaped, axis, 0, 0, tiled=True).reshape(block.shape)


def per_device(
    state,
    propeller,
    donor_index,
    fringe_index,
    donor_weight,
    disk_mask,
    thrust,
    face,
    coupling,
    diag_inverse,
    lower_jacobian,
    upper_jacobian,
):
    donors = pl.pallas_call(
        donor_kernel,
        out_shape=jax.ShapeDtypeStruct((GIRTHS * DONOR_ROWS, 128), F32),
        in_specs=[VMEM] * 5,
        out_specs=VMEM,
        name="donors",
    )(propeller, donor_index, fringe_index, donor_weight, state.reshape(112, 128))
    landed = exchange(donors, "girth", GIRTHS)
    send, current = pl.pallas_call(
        flow_kernel,
        out_shape=(
            jax.ShapeDtypeStruct((STREAMS * SEND_ROWS, 128), F32),
            jax.ShapeDtypeStruct(state.shape, F32),
        ),
        in_specs=[VMEM] * 5 + [SMEM] * 2,
        out_specs=(VMEM, VMEM),
        name="flow",
    )(landed, state, face, disk_mask, diag_inverse, thrust, coupling)
    moved = exchange(send, "stream", STREAMS)
    back = pl.pallas_call(
        solve_kernel,
        out_shape=jax.ShapeDtypeStruct((STREAMS * BACK_ROWS, 128), F32),
        in_specs=[VMEM] + [SMEM] * 3,
        out_specs=VMEM,
        scratch_shapes=[
            pltpu.VMEM((2, 49, 8, 128), F32),
            pltpu.VMEM((2, 49, 8, 128), F32),
            pltpu.VMEM((2, 49, 8, 128), F32),
            pltpu.VMEM((3, 49, 8, 128), F32),
            pltpu.VMEM((49, 8, 128), F32),
        ],
        name="solve",
    )(moved, coupling, lower_jacobian, upper_jacobian)
    returned = exchange(back, "stream", STREAMS)
    return pl.pallas_call(
        finish_kernel,
        out_shape=(
            jax.ShapeDtypeStruct(state.shape, F32),
            jax.ShapeDtypeStruct(state.shape, F32),
        ),
        in_specs=[VMEM] * 2,
        out_specs=(VMEM, VMEM),
        name="finish",
    )(returned, current)


def solution(mesh):
    placed = (
        P("stream", None, "girth", None),
        P(None, ("stream", "girth")),
        P(("stream", "girth"), None),
        P(("stream", "girth"), None),
        P(("stream", "girth"), None),
        P("stream", "girth", None),
        P(),
        P("stream", None, "girth", None),
        P(),
        P("stream", None, None, "girth", None),
        P(),
        P(),
    )
    return jax.shard_map(
        per_device,
        mesh=mesh,
        in_specs=placed,
        out_specs=(P("stream", None, "girth", None), P("stream", None, "girth", None)),
        check_vma=False,
    )
```

```python
import jax
import jax.numpy as jnp
from jax import lax
from jax.experimental import pallas as pl
from jax.experimental.pallas import tpu as pltpu
from jax.sharding import PartitionSpec as P

F32 = jnp.float32
BF16 = jnp.bfloat16
VARS = 7
STREAMS = 32
GIRTHS = 16
DONOR_ROWS = 24
SEND_ROWS = 33
BACK_ROWS = 7
FLOW_VALUES = 32


def lanes(shape=(8, 128)):
    return lax.broadcasted_iota(jnp.int32, shape, len(shape) - 1)


def sublanes(shape=(8, 128)):
    return lax.broadcasted_iota(jnp.int32, shape, len(shape) - 2)


def split_parts(x):
    high = x.astype(BF16).astype(F32)
    rest = x - high
    middle = rest.astype(BF16).astype(F32)
    return high, middle, rest - middle


def block_transpose(a, b, c, d):
    lane = lanes()
    half = lane < 64
    even = (lane & 32) == 0
    a, c = jnp.where(half, a, pltpu.roll(c, 64, 1)), jnp.where(half, pltpu.roll(a, 64, 1), c)
    b, d = jnp.where(half, b, pltpu.roll(d, 64, 1)), jnp.where(half, pltpu.roll(b, 64, 1), d)
    a, b = jnp.where(even, a, pltpu.roll(b, 32, 1)), jnp.where(even, pltpu.roll(a, 96, 1), b)
    c, d = jnp.where(even, c, pltpu.roll(d, 32, 1)), jnp.where(even, pltpu.roll(c, 96, 1), d)
    return a, b, c, d


def donor_kernel(prop_ref, index_ref, fringe_ref, weight_ref, state_ref, out_ref):
    place = lax.axis_index("girth")
    index = index_ref[...]
    cells = lax.broadcasted_iota(jnp.int32, (256, 128), 0)
    pick = jnp.where(cells == index, 1.0, 0.0).astype(BF16)
    values = jnp.zeros((VARS, 128), F32)
    for part in split_parts(prop_ref[...]):
        values = values + jnp.dot(part.astype(BF16), pick, preferred_element_type=F32)
    values = values * weight_ref[...]
    target = jnp.where(index >= 0, fringe_ref[...], -1).astype(F32)
    edges = [
        (
            state_ref[pl.ds(row * 56, VARS, stride=8), :],
            state_ref[pl.ds(row * 56 + 7, VARS, stride=8), :],
        )
        for row in range(2)
    ]
    upper = lax.rem(place + 1, GIRTHS)
    for peer in range(GIRTHS):
        start = peer * DONOR_ROWS
        out_ref[start : start + VARS, :] = values
        out_ref[start + VARS : start + 8, :] = target
        out_ref[start + 8 : start + 24, :] = jnp.zeros((16, 128), F32)
        for row, (first, last) in enumerate(edges):
            at = start + 8 + row * 8
            out_ref[at : at + VARS, :] = jnp.where(upper == peer, last, first)


def fringe_sums(landed_ref, place):
    sub, lane = sublanes(), lanes()
    row = lanes((1, 128))
    slot = row & 31
    left = {}
    right = []
    for group in range(4):
        entries = jnp.zeros((8, 128), F32)
        for quarter in range(4):
            sender = group * 4 + quarter
            shift = lax.rem(32 * quarter + 8 - 8 * place + 128, 128)
            rolled = pltpu.roll(landed_ref[sender * DONOR_ROWS : sender * DONOR_ROWS + 8, :], shift, 1)
            entries = jnp.where((lane >> 5) == quarter, rolled, entries)
        target = entries[7:8, :].astype(jnp.int32)
        live = target >= 0
        tall = target >> 7
        own = jnp.where(live & (slot >= 8) & (slot < 16), tall, -1)
        low = jnp.where(live & (slot < 8) & ((tall & 7) == 7), tall >> 3, -1)
        high = jnp.where(live & (slot >= 16) & (slot < 24) & ((tall & 7) == 0), tall >> 3, -1)
        onto = lax.broadcasted_iota(jnp.int32, (128, 128), 0)
        right.append(jnp.where(onto == (target & 127), 1.0, 0.0).astype(BF16))
        parts = split_parts(entries)
        for which, part in enumerate(parts):
            counted = 1.0 if which == 0 else 0.0
            marked = jnp.where(sub == 7, counted, part)
            rows = []
            for r in range(2):
                inside = own == sub + 8 * r
                for v in range(8):
                    rows.append(jnp.where(inside, marked[v : v + 1, :], 0.0))
            for side in (low, high):
                for r in range(2):
                    rows.append(jnp.where(side == r, marked, 0.0))
            left[which, group] = jnp.concatenate(rows, axis=0).astype(BF16)
    right = jnp.concatenate(right, axis=1)
    total = None
    for which in range(3):
        lhs = jnp.concatenate([left[which, group] for group in range(4)], axis=1)
        part = lax.dot_general(lhs, right, (((1,), (1,)), ((), ())), preferred_element_type=F32)
        total = part if total is None else total + part
    return total


def flow_kernel(
    landed_ref,
    state_ref,
    face_ref,
    disk_ref,
    diag_ref,
    thrust_ref,
    coupling_ref,
    send_ref,
    current_ref,
):
    place = lax.axis_index("girth")
    sub, lane = sublanes(), lanes()
    sums = fringe_sums(landed_ref, place)
    edges = []
    for side, peer in enumerate((lax.rem(place + 15, GIRTHS), lax.rem(place + 1, GIRTHS))):
        both = []
        for r in range(2):
            start = pl.multiple_of(peer * DONOR_ROWS + 8 + 8 * r, 8)
            edge = landed_ref[pl.ds(start, 8), :]
            found = sums[128 + side * 16 + r * 8 : 136 + side * 16 + r * 8, :]
            both.append(jnp.where(found[7:8, :] > 0.5, found, edge))
        edges.append(both)
    current, fringe = [], []
    for r in range(2):
        block = sums[r * 64 : (r + 1) * 64, :]
        hit = block[56:64, :] > 0.5
        fringe.append(hit)
        current.append(
            [jnp.where(hit, block[v * 8 : v * 8 + 8, :], state_ref[r, v]) for v in range(VARS)]
        )
    zero = jnp.zeros((8, 128), F32)
    residual = []
    for r in range(2):
        own = current[r]
        disk = disk_ref[r].astype(F32)
        total = [disk * thrust_ref[i] for i in range(VARS)]
        for direction in range(6):
            if direction == 0:
                beside = current[0] if r == 1 else [zero] * VARS
            elif direction == 1:
                beside = current[1] if r == 0 else [zero] * VARS
            elif direction == 2:
                beside = [
                    jnp.where(sub == 0, edges[0][r][v : v + 1, :], pltpu.roll(own[v], 1, 0))
                    for v in range(VARS)
                ]
            elif direction == 3:
                beside = [
                    jnp.where(sub == 7, edges[1][r][v : v + 1, :], pltpu.roll(own[v], 7, 0))
                    for v in range(VARS)
                ]
            elif direction == 4:
                beside = [jnp.where(lane == 0, 0.0, pltpu.roll(own[v], 1, 1)) for v in range(VARS)]
            else:
                beside = [
                    jnp.where(lane == 127, 0.0, pltpu.roll(own[v], 127, 1)) for v in range(VARS)
                ]
            factor = face_ref[r, direction]
            jump = [factor * (beside[v] - own[v]) for v in range(VARS)]
            for i in range(VARS):
                for j in range(VARS):
                    total[i] = total[i] + coupling_ref[direction, i, j] * jump[j]
        residual.append(total)
        for v in range(VARS):
            current_ref[r, v] = own[v]

    def pack(k, four):
        for quarter, tile in enumerate(block_transpose(*four)):
            send_ref[pl.ds(quarter * 8 * SEND_ROWS + k, 8, stride=SEND_ROWS), :] = tile

    flow = residual[0] + residual[1] + current[0] + current[1]
    flow += [jnp.where(hit, 1.0, 0.0) for hit in fringe]
    flow += [face_ref[0, 0], face_ref[1, 1]]
    for k in range(FLOW_VALUES // 4):
        pack(k, flow[4 * k : 4 * k + 4])
    places = [(r, i, j) for r in range(2) for i in range(VARS) for j in range(VARS)]
    for k in range(25):
        four = [diag_ref[at].astype(F32) for at in places[4 * k : 4 * k + 4]]
        pack(FLOW_VALUES // 4 + k, four + [zero] * (4 - len(four)))


def from_before(x, count):
    sub, lane = sublanes(), lanes()
    if count == 4:
        return jnp.where(sub == 0, 0.0, pltpu.roll(x, 1, 0))
    width = 32 * count
    x = pltpu.roll(x, width, 1)
    return jnp.where(lane < width, jnp.where(sub == 0, 0.0, pltpu.roll(x, 1, 0)), x)


def from_after(x, count):
    sub, lane = sublanes(), lanes()
    if count == 4:
        return jnp.where(sub == 7, 0.0, pltpu.roll(x, 7, 0))
    width = 32 * count
    x = pltpu.roll(x, 128 - width, 1)
    return jnp.where(lane >= 128 - width, jnp.where(sub == 7, 0.0, pltpu.roll(x, 7, 0)), x)


def total_of(terms):
    while len(terms) > 1:
        terms = [sum(terms[at : at + 2]) for at in range(0, len(terms), 2)]
    return terms[0]


def apply(ref, vector, add=None):
    result = []
    for i in range(VARS):
        terms = [ref[i * VARS + j] * vector[j] for j in range(VARS)]
        result.append(total_of(terms + ([add[i]] if add is not None else [])))
    return result


def solve_kernel(
    moved_ref, coupling_ref, lower_ref, upper_ref, back_ref, diag, near, far, maps, moved_maps
):
    def unpack(k):
        return block_transpose(
            *[
                moved_ref[pl.ds(quarter * SEND_ROWS + k, 8, stride=4 * SEND_ROWS), :]
                for quarter in range(4)
            ]
        )

    flow = []
    for k in range(FLOW_VALUES // 4):
        flow += unpack(k)
    for k in range(25):
        for at, tile in enumerate(unpack(FLOW_VALUES // 4 + k)):
            if 4 * k + at < 98:
                diag[(4 * k + at) // 49, (4 * k + at) % 49] = tile
    residual = [flow[0:7], flow[7:14]]
    current = [flow[14:21], flow[21:28]]
    fringe = [flow[28] > 0.5, flow[29] > 0.5]
    factors = flow[30:32]
    beside = [
        [factors[0] * from_before(current[1][v], 1) for v in range(VARS)],
        [factors[1] * from_after(current[0][v], 1) for v in range(VARS)],
    ]
    for r in range(2):
        for i in range(VARS):
            for j in range(VARS):
                residual[r][i] = residual[r][i] + coupling_ref[r, i, j] * beside[r][j]
    source = [[jnp.where(fringe[r], 0.0, -residual[r][i]) for i in range(VARS)] for r in range(2)]

    def times(matrix_ref, out):
        for r in range(2):
            for i in range(VARS):
                row = [diag[r, i * VARS + j] for j in range(VARS)]
                for k in range(VARS):
                    out[r, i * VARS + k] = total_of(
                        [row[j] * matrix_ref[j, k] for j in range(VARS)]
                    )

    def multiply(a, b, out):
        for i in range(VARS):
            row = [a[i * VARS + j] for j in range(VARS)]
            for k in range(VARS):
                out[i * VARS + k] = total_of([row[j] * b[j * VARS + k] for j in range(VARS)])

    def scan(offset, shifted):
        for level, count in enumerate((1, 2)):
            a = maps.at[level]
            for at in range(49):
                moved_maps[at] = shifted(a[at], count)
            offset = apply(a, [shifted(x, count) for x in offset], offset)
            multiply(a, moved_maps, maps.at[level + 1])
        a = maps.at[2]
        x = offset
        for _ in range(7):
            x = apply(a, [shifted(part, 4) for part in x], offset)
        return x

    times(lower_ref, near)
    times(upper_ref, far)
    first = apply(diag.at[0], source[0])
    second = apply(near.at[1], first, apply(diag.at[1], source[1]))
    multiply(near.at[1], near.at[0], maps.at[0])
    second = scan(second, from_before)
    first = apply(near.at[0], [from_before(x, 1) for x in second], first)
    multiply(far.at[0], far.at[1], maps.at[0])
    update_first = scan(apply(far.at[0], second, first), from_after)
    update_second = apply(far.at[1], [from_after(x, 1) for x in update_first], second)

    results = update_first + update_second + residual[0] + residual[1]
    for k in range(BACK_ROWS):
        for quarter, tile in enumerate(block_transpose(*results[4 * k : 4 * k + 4])):
            back_ref[pl.ds(quarter * BACK_ROWS + k, 8, stride=4 * BACK_ROWS), :] = tile


def finish_kernel(returned_ref, current_ref, state_ref, residual_ref):
    results = []
    for k in range(BACK_ROWS):
        results += block_transpose(
            *[
                returned_ref[pl.ds(quarter * 8 * BACK_ROWS + k, 8, stride=BACK_ROWS), :]
                for quarter in range(4)
            ]
        )
    for r in range(2):
        for v in range(VARS):
            state_ref[r, v] = current_ref[r, v] + results[r * VARS + v]
            residual_ref[r, v] = results[14 + r * VARS + v]


VMEM = pl.BlockSpec(memory_space=pltpu.VMEM)
SMEM = pl.BlockSpec(memory_space=pltpu.SMEM)


def exchange(block, axis, parts):
    rows = block.shape[0] // parts
    if rows % 8 == 0:
        shaped = block.reshape(parts, rows, 128)
    else:
        shaped = block.reshape(block.shape[0], 1, 128)
    return lax.all_to_all(shaped, axis, 0, 0, tiled=True).reshape(block.shape)


def per_device(
    state,
    propeller,
    donor_index,
    fringe_index,
    donor_weight,
    disk_mask,
    thrust,
    face,
    coupling,
    diag_inverse,
    lower_jacobian,
    upper_jacobian,
):
    donors = pl.pallas_call(
        donor_kernel,
        out_shape=jax.ShapeDtypeStruct((GIRTHS * DONOR_ROWS, 128), F32),
        in_specs=[VMEM] * 5,
        out_specs=VMEM,
        compiler_params=pltpu.CompilerParams(vmem_limit_bytes=4 << 20),
        name="donors",
    )(propeller, donor_index, fringe_index, donor_weight, state.reshape(112, 128))
    landed = exchange(donors, "girth", GIRTHS)
    send, current = pl.pallas_call(
        flow_kernel,
        out_shape=(
            jax.ShapeDtypeStruct((STREAMS * SEND_ROWS, 128), F32),
            jax.ShapeDtypeStruct(state.shape, F32),
        ),
        in_specs=[VMEM] * 5 + [SMEM] * 2,
        out_specs=(VMEM, VMEM),
        compiler_params=pltpu.CompilerParams(vmem_limit_bytes=16 << 20),
        name="flow",
    )(landed, state, face, disk_mask, diag_inverse, thrust, coupling)
    moved = exchange(send, "stream", STREAMS)
    back = pl.pallas_call(
        solve_kernel,
        out_shape=jax.ShapeDtypeStruct((STREAMS * BACK_ROWS, 128), F32),
        in_specs=[VMEM] + [SMEM] * 3,
        out_specs=VMEM,
        scratch_shapes=[
            pltpu.VMEM((2, 49, 8, 128), F32),
            pltpu.VMEM((2, 49, 8, 128), F32),
            pltpu.VMEM((2, 49, 8, 128), F32),
            pltpu.VMEM((3, 49, 8, 128), F32),
            pltpu.VMEM((49, 8, 128), F32),
        ],
        compiler_params=pltpu.CompilerParams(vmem_limit_bytes=16 << 20),
        name="solve",
    )(moved, coupling, lower_jacobian, upper_jacobian)
    returned = exchange(back, "stream", STREAMS)
    return pl.pallas_call(
        finish_kernel,
        out_shape=(
            jax.ShapeDtypeStruct(state.shape, F32),
            jax.ShapeDtypeStruct(state.shape, F32),
        ),
        in_specs=[VMEM] * 2,
        out_specs=(VMEM, VMEM),
        compiler_params=pltpu.CompilerParams(vmem_limit_bytes=4 << 20),
        name="finish",
    )(returned, current)


def solution(mesh):
    placed = (
        P("stream", None, "girth", None),
        P(None, ("stream", "girth")),
        P(("stream", "girth"), None),
        P(("stream", "girth"), None),
        P(("stream", "girth"), None),
        P("stream", "girth", None),
        P(),
        P("stream", None, "girth", None),
        P(),
        P("stream", None, None, "girth", None),
        P(),
        P(),
    )
    return jax.shard_map(
        per_device,
        mesh=mesh,
        in_specs=placed,
        out_specs=(P("stream", None, "girth", None), P("stream", None, "girth", None)),
        check_vma=False,
    )
```

```python
import jax
import jax.numpy as jnp
from jax import lax
from jax.experimental import pallas as pl
from jax.experimental.pallas import tpu as pltpu
from jax.sharding import PartitionSpec as P

F32 = jnp.float32
BF16 = jnp.bfloat16
VARS = 7
STREAMS = 32
GIRTHS = 16
DONOR_ROWS = 24
SEND_ROWS = 32
BACK_ROWS = 4


def lanes(shape=(8, 128)):
    return lax.broadcasted_iota(jnp.int32, shape, len(shape) - 1)


def sublanes(shape=(8, 128)):
    return lax.broadcasted_iota(jnp.int32, shape, len(shape) - 2)


def split_parts(x):
    high = x.astype(BF16).astype(F32)
    rest = x - high
    middle = rest.astype(BF16).astype(F32)
    return high, middle, rest - middle


def block_transpose(a, b, c, d):
    lane = lanes()
    half = lane < 64
    even = (lane & 32) == 0
    a, c = jnp.where(half, a, pltpu.roll(c, 64, 1)), jnp.where(half, pltpu.roll(a, 64, 1), c)
    b, d = jnp.where(half, b, pltpu.roll(d, 64, 1)), jnp.where(half, pltpu.roll(b, 64, 1), d)
    a, b = jnp.where(even, a, pltpu.roll(b, 32, 1)), jnp.where(even, pltpu.roll(a, 96, 1), b)
    c, d = jnp.where(even, c, pltpu.roll(d, 32, 1)), jnp.where(even, pltpu.roll(c, 96, 1), d)
    return a, b, c, d


def pack(tiles, store):
    for first in range(0, len(tiles) // 4, 8):
        rows = [block_transpose(*tiles[4 * k : 4 * k + 4]) for k in range(first, first + 8)]
        for quarter in range(4):
            turned = jnp.swapaxes(jnp.stack([four[quarter] for four in rows]), 0, 1)
            for g in range(8):
                store[quarter * 8 + g, first : first + 8, :] = turned[g]


def donor_kernel(
    prop_hbm,
    index_hbm,
    fringe_hbm,
    weight_hbm,
    state_hbm,
    thrust_hbm,
    out_ref,
    thrust_out,
    prop_ref,
    index_ref,
    fringe_ref,
    weight_ref,
    state_ref,
    thrust_ref,
    sems,
):
    copies = [
        pltpu.make_async_copy(source, target, sems.at[at])
        for at, (source, target) in enumerate(
            (
                (index_hbm, index_ref),
                (prop_hbm, prop_ref),
                (weight_hbm, weight_ref),
                (fringe_hbm, fringe_ref),
                (state_hbm, state_ref),
                (thrust_hbm, thrust_ref),
            )
        )
    ]
    for copy in copies:
        copy.start()
    for copy in copies:
        copy.wait()
    for v in range(VARS):
        thrust_out[v] = jnp.full((8, 128), thrust_ref[v], F32)
    place = lax.axis_index("girth")
    index = index_ref[...]
    cells = lax.broadcasted_iota(jnp.int32, (256, 128), 0)
    pick = jnp.where(cells == index, 1.0, 0.0).astype(BF16)
    values = jnp.zeros((VARS, 128), F32)
    for part in split_parts(prop_ref[...]):
        values = values + jnp.dot(part.astype(BF16), pick, preferred_element_type=F32)
    values = values * weight_ref[...]
    target = jnp.where(index >= 0, fringe_ref[...], -1).astype(F32)
    edges = [
        (
            state_ref[pl.ds(row * 56, VARS, stride=8), :],
            state_ref[pl.ds(row * 56 + 7, VARS, stride=8), :],
        )
        for row in range(2)
    ]
    upper = lax.rem(place + 1, GIRTHS)
    for peer in range(GIRTHS):
        start = peer * DONOR_ROWS
        out_ref[start : start + VARS, :] = values
        out_ref[start + VARS : start + 8, :] = target
        out_ref[start + 8 : start + 24, :] = jnp.zeros((16, 128), F32)
        for row, (first, last) in enumerate(edges):
            at = start + 8 + row * 8
            out_ref[at : at + VARS, :] = jnp.where(upper == peer, last, first)


def fringe_sums(landed_ref, place):
    sub, lane = sublanes(), lanes()
    row = lanes((1, 128))
    slot = row & 31
    left = {}
    right = []
    for group in range(4):
        entries = jnp.zeros((8, 128), F32)
        for quarter in range(4):
            sender = group * 4 + quarter
            shift = lax.rem(32 * quarter + 8 - 8 * place + 128, 128)
            rolled = pltpu.roll(landed_ref[sender * DONOR_ROWS : sender * DONOR_ROWS + 8, :], shift, 1)
            entries = jnp.where((lane >> 5) == quarter, rolled, entries)
        target = entries[7:8, :].astype(jnp.int32)
        live = target >= 0
        tall = target >> 7
        own = jnp.where(live & (slot >= 8) & (slot < 16), tall, -1)
        low = jnp.where(live & (slot < 8) & ((tall & 7) == 7), tall >> 3, -1)
        high = jnp.where(live & (slot >= 16) & (slot < 24) & ((tall & 7) == 0), tall >> 3, -1)
        onto = lax.broadcasted_iota(jnp.int32, (128, 128), 0)
        right.append(jnp.where(onto == (target & 127), 1.0, 0.0).astype(BF16))
        parts = split_parts(entries)
        for which, part in enumerate(parts):
            counted = 1.0 if which == 0 else 0.0
            marked = jnp.where(sub == 7, counted, part)
            rows = []
            for r in range(2):
                inside = own == sub + 8 * r
                for v in range(8):
                    rows.append(jnp.where(inside, marked[v : v + 1, :], 0.0))
            for side in (low, high):
                for r in range(2):
                    rows.append(jnp.where(side == r, marked, 0.0))
            left[which, group] = jnp.concatenate(rows, axis=0).astype(BF16)
    right = jnp.concatenate(right, axis=1)
    total = None
    for which in range(3):
        lhs = jnp.concatenate([left[which, group] for group in range(4)], axis=1)
        part = lax.dot_general(lhs, right, (((1,), (1,)), ((), ())), preferred_element_type=F32)
        total = part if total is None else total + part
    return total


def flow_kernel(
    landed_ref,
    state_ref,
    face_ref,
    disk_ref,
    diag_ref,
    thrust_ref,
    coupling_ref,
    send_ref,
    current_ref,
    down_ref,
    up_ref,
    partial_ref,
    factor_ref,
    diag_rows,
    flow_rows,
    sems,
):
    tiles = [
        diag_ref[r, i, j].astype(F32) for r in range(2) for i in range(VARS) for j in range(VARS)
    ]
    pack(tiles[2:], diag_rows)
    diag_copy = pltpu.make_async_copy(diag_rows, send_ref.at[:, 8:, :], sems.at[0])
    diag_copy.start()
    place = lax.axis_index("girth")
    sub, lane = sublanes(), lanes()
    sums = fringe_sums(landed_ref, place)
    edges = []
    for side, peer in enumerate((lax.rem(place + 15, GIRTHS), lax.rem(place + 1, GIRTHS))):
        both = []
        for r in range(2):
            start = pl.multiple_of(peer * DONOR_ROWS + 8 + 8 * r, 8)
            edge = landed_ref[pl.ds(start, 8), :]
            found = sums[128 + side * 16 + r * 8 : 136 + side * 16 + r * 8, :]
            both.append(jnp.where(found[7:8, :] > 0.5, found, edge))
        edges.append(both)
    current, fringe = [], []
    for r in range(2):
        block = sums[r * 64 : (r + 1) * 64, :]
        hit = block[56:64, :] > 0.5
        fringe.append(hit)
        current.append(
            [jnp.where(hit, block[v * 8 : v * 8 + 8, :], state_ref[r, v]) for v in range(VARS)]
        )
    zero = jnp.zeros((8, 128), F32)
    residual = []
    for r in range(2):
        disk = disk_ref[r].astype(F32)
        residual.append([disk * thrust_ref[i] for i in range(VARS)])
    for direction in range(6):
        jumps = []
        for r in range(2):
            own = current[r]
            if direction < 2:
                beside = [zero] * VARS if direction == r else current[1 - r]
            elif direction == 2:
                beside = [
                    jnp.where(sub == 0, edges[0][r][v : v + 1, :], pltpu.roll(own[v], 1, 0))
                    for v in range(VARS)
                ]
            elif direction == 3:
                beside = [
                    jnp.where(sub == 7, edges[1][r][v : v + 1, :], pltpu.roll(own[v], 7, 0))
                    for v in range(VARS)
                ]
            elif direction == 4:
                beside = [jnp.where(lane == 0, 0.0, pltpu.roll(own[v], 1, 1)) for v in range(VARS)]
            else:
                beside = [
                    jnp.where(lane == 127, 0.0, pltpu.roll(own[v], 127, 1)) for v in range(VARS)
                ]
            factor = face_ref[r, direction]
            jumps.append([factor * (beside[v] - own[v]) for v in range(VARS)])
        for i in range(VARS):
            for j in range(VARS):
                weight = coupling_ref[direction, i, j]
                for r in range(2):
                    residual[r][i] = residual[r][i] + weight * jumps[r][j]
    factors = [face_ref[r, r] for r in range(2)]
    passed = []
    for r, ref in enumerate((down_ref, up_ref)):
        passed += [
            total_of([coupling_ref[r, i, j] * current[1 - r][j] for j in range(VARS)])
            for i in range(VARS)
        ]
        factor_ref[r] = factors[r]
        for v in range(VARS):
            ref[v] = passed[r * VARS + v]
            current_ref[r, v] = current[r][v]
            partial_ref[r, v] = residual[r][v]
    flow = [jnp.where(fringe[r], 0.0, x) for r in range(2) for x in residual[r]]
    flow += passed
    flow += [jnp.where(fringe[r], 0.0, factors[r]) for r in range(2)]
    flow += [diag_ref[0, 0, j].astype(F32) for j in range(2)]
    pack(flow, flow_rows)
    flow_copy = pltpu.make_async_copy(flow_rows, send_ref.at[:, :8, :], sems.at[1])
    flow_copy.start()
    flow_copy.wait()
    diag_copy.wait()


def from_before(x, count):
    sub, lane = sublanes(), lanes()
    wrapped = jnp.where(lane < 32, 0.0, pltpu.roll(x, 32, 1))
    if count == 8:
        return wrapped
    return jnp.where(sub < count, pltpu.roll(wrapped, count, 0), pltpu.roll(x, count, 0))


def from_after(x, count):
    sub, lane = sublanes(), lanes()
    wrapped = jnp.where(lane >= 96, 0.0, pltpu.roll(x, 96, 1))
    if count == 8:
        return wrapped
    return jnp.where(
        sub >= 8 - count, pltpu.roll(wrapped, 8 - count, 0), pltpu.roll(x, 8 - count, 0)
    )


def total_of(terms):
    while len(terms) > 1:
        terms = [sum(terms[at : at + 2]) for at in range(0, len(terms), 2)]
    return terms[0]


def apply(ref, vector, add=None):
    result = []
    for i in range(VARS):
        terms = [ref[i * VARS + j] * vector[j] for j in range(VARS)]
        result.append(total_of(terms + ([add[i]] if add is not None else [])))
    return result


def solve_kernel(
    moved_ref, lower_ref, upper_ref, back_ref, diag, near, far, maps, moved_maps
):
    flow = []
    for first in range(0, SEND_ROWS, 8):
        tiles = []
        for quarter in range(4):
            loaded = [moved_ref[quarter * 8 + s, first : first + 8, :] for s in range(8)]
            tiles.append(jnp.swapaxes(jnp.stack(loaded), 0, 1))
        for k in range(8):
            for at, tile in enumerate(block_transpose(*[four[k] for four in tiles])):
                place = 4 * (first + k) + at - 30
                if place < 0:
                    flow.append(tile)
                else:
                    diag[place // 49, place % 49] = tile
    beside = [
        [from_before(flow[14 + v], 1) for v in range(VARS)],
        [from_after(flow[21 + v], 1) for v in range(VARS)],
    ]
    source = [
        [-flow[r * VARS + i] - flow[28 + r] * beside[r][i] for i in range(VARS)] for r in range(2)
    ]

    def times(matrix_ref, out):
        for k in range(VARS):
            column = [jnp.full((8, 128), matrix_ref[j, k], F32) for j in range(VARS)]
            for r in range(2):
                for i in range(VARS):
                    out[r, i * VARS + k] = total_of(
                        [diag[r, i * VARS + j] * column[j] for j in range(VARS)]
                    )

    def multiply(a, b, out):
        for i in range(VARS):
            row = [a[i * VARS + j] for j in range(VARS)]
            for k in range(VARS):
                out[i * VARS + k] = total_of([row[j] * b[j * VARS + k] for j in range(VARS)])

    def scan(offset, shifted):
        for level, count in enumerate((1, 2, 4)):
            a = maps.at[level]
            for at in range(49):
                moved_maps[at] = shifted(a[at], count)
            offset = apply(a, [shifted(x, count) for x in offset], offset)
            multiply(a, moved_maps, maps.at[level + 1])
        a = maps.at[3]
        x = offset
        for _ in range(3):
            x = apply(a, [shifted(part, 8) for part in x], offset)
        return x

    times(lower_ref, near)
    times(upper_ref, far)
    first = apply(diag.at[0], source[0])
    second = apply(near.at[1], first, apply(diag.at[1], source[1]))
    multiply(near.at[1], near.at[0], maps.at[0])
    second = scan(second, from_before)
    first = apply(near.at[0], [from_before(x, 1) for x in second], first)
    multiply(far.at[0], far.at[1], maps.at[0])
    update_first = scan(apply(far.at[0], second, first), from_after)
    update_second = apply(far.at[1], [from_after(x, 1) for x in update_first], second)

    results = update_first + update_second + [jnp.zeros((8, 128), F32)] * 2
    for k in range(BACK_ROWS):
        for quarter, tile in enumerate(block_transpose(*results[4 * k : 4 * k + 4])):
            back_ref[pl.ds(quarter * 8 * BACK_ROWS + k, 8, stride=BACK_ROWS), :] = tile


def finish_kernel(
    returned_ref, current_ref, partial_ref, factor_ref, low_ref, high_ref, state_ref, residual_ref
):
    results = []
    for k in range(BACK_ROWS):
        results += block_transpose(
            *[
                returned_ref[pl.ds(quarter * 8 * BACK_ROWS + k, 8, stride=BACK_ROWS), :]
                for quarter in range(4)
            ]
        )
    for r, ref in enumerate((low_ref, high_ref)):
        for v in range(VARS):
            state_ref[r, v] = current_ref[r, v] + results[r * VARS + v]
            residual_ref[r, v] = partial_ref[r, v] + factor_ref[r] * ref[v]


VMEM = pl.BlockSpec(memory_space=pltpu.VMEM)
SMEM = pl.BlockSpec(memory_space=pltpu.SMEM)
HBM = pl.BlockSpec(memory_space=pltpu.HBM)


def exchange(block, axis, parts):
    rows = block.shape[0] // parts
    shaped = block.reshape(parts, rows, 128)
    return lax.all_to_all(shaped, axis, 0, 0, tiled=True).reshape(block.shape)


def per_device(
    state,
    propeller,
    donor_index,
    fringe_index,
    donor_weight,
    disk_mask,
    thrust,
    face,
    coupling,
    diag_inverse,
    lower_jacobian,
    upper_jacobian,
):
    inputs = (propeller, donor_index, fringe_index, donor_weight, state.reshape(112, 128), thrust)
    inputs = [pltpu.with_memory_space_constraint(x, pltpu.HBM) for x in inputs]
    donors, thrusts = pl.pallas_call(
        donor_kernel,
        out_shape=(
            jax.ShapeDtypeStruct((GIRTHS * DONOR_ROWS, 128), F32),
            jax.ShapeDtypeStruct((VARS, 8, 128), F32),
        ),
        in_specs=[HBM] * 6,
        out_specs=(VMEM, VMEM),
        scratch_shapes=[
            pltpu.VMEM((VARS, 256), F32),
            pltpu.VMEM((1, 128), jnp.int32),
            pltpu.VMEM((1, 128), jnp.int32),
            pltpu.VMEM((1, 128), F32),
            pltpu.VMEM((112, 128), F32),
            pltpu.SMEM((VARS,), F32),
            pltpu.SemaphoreType.DMA((6,)),
        ],
        compiler_params=pltpu.CompilerParams(vmem_limit_bytes=4 << 20),
        name="donors",
    )(*inputs)
    landed = exchange(donors, "girth", GIRTHS)
    row = jax.ShapeDtypeStruct(state.shape[1:], F32)
    both = jax.ShapeDtypeStruct(state.shape, F32)
    send, current, down, up, partial, factor = pl.pallas_call(
        flow_kernel,
        out_shape=(
            jax.ShapeDtypeStruct((STREAMS, SEND_ROWS, 128), F32),
            both,
            row,
            row,
            both,
            jax.ShapeDtypeStruct((2, 8, 128), F32),
        ),
        in_specs=[VMEM] * 6 + [SMEM],
        out_specs=(pl.BlockSpec(memory_space=pl.ANY),) + (VMEM,) * 5,
        scratch_shapes=[
            pltpu.VMEM((STREAMS, SEND_ROWS - 8, 128), F32),
            pltpu.VMEM((STREAMS, 8, 128), F32),
            pltpu.SemaphoreType.DMA((2,)),
        ],
        compiler_params=pltpu.CompilerParams(vmem_limit_bytes=16 << 20),
        name="flow",
    )(landed, state, face, disk_mask, diag_inverse, thrusts, coupling)
    moved = lax.all_to_all(send, "stream", 0, 0, tiled=True)
    ahead = [(at, at + 1) for at in range(STREAMS - 1)]
    low = lax.ppermute(down, "stream", ahead)
    high = lax.ppermute(up, "stream", [(b, a) for a, b in ahead])
    back = pl.pallas_call(
        solve_kernel,
        out_shape=jax.ShapeDtypeStruct((STREAMS * BACK_ROWS, 128), F32),
        in_specs=[VMEM] + [SMEM] * 2,
        out_specs=VMEM,
        scratch_shapes=[
            pltpu.VMEM((2, 49, 8, 128), F32),
            pltpu.VMEM((2, 49, 8, 128), F32),
            pltpu.VMEM((2, 49, 8, 128), F32),
            pltpu.VMEM((4, 49, 8, 128), F32),
            pltpu.VMEM((49, 8, 128), F32),
        ],
        compiler_params=pltpu.CompilerParams(vmem_limit_bytes=16 << 20),
        name="solve",
    )(moved, lower_jacobian, upper_jacobian)
    back, low, high = lax.optimization_barrier((back, low, high))
    returned = exchange(back, "stream", STREAMS)
    return pl.pallas_call(
        finish_kernel,
        out_shape=(both, both),
        in_specs=[VMEM] * 6,
        out_specs=(VMEM, VMEM),
        compiler_params=pltpu.CompilerParams(vmem_limit_bytes=4 << 20),
        name="finish",
    )(returned, current, partial, factor, low, high)


def solution(mesh):
    placed = (
        P("stream", None, "girth", None),
        P(None, ("stream", "girth")),
        P(("stream", "girth"), None),
        P(("stream", "girth"), None),
        P(("stream", "girth"), None),
        P("stream", "girth", None),
        P(),
        P("stream", None, "girth", None),
        P(),
        P("stream", None, None, "girth", None),
        P(),
        P(),
    )
    return jax.shard_map(
        per_device,
        mesh=mesh,
        in_specs=placed,
        out_specs=(P("stream", None, "girth", None), P("stream", None, "girth", None)),
        check_vma=False,
    )
```

```python
import jax
import jax.numpy as jnp
from jax import lax
from jax.experimental import pallas as pl
from jax.experimental.pallas import tpu as pltpu
from jax.sharding import PartitionSpec as P

F32 = jnp.float32
BF16 = jnp.bfloat16
VARS = 7
STREAMS = 32
GIRTHS = 16
DONOR_ROWS = 24
SEND_ROWS = 32
BACK_ROWS = 4


def lanes(shape=(8, 128)):
    return lax.broadcasted_iota(jnp.int32, shape, len(shape) - 1)


def sublanes(shape=(8, 128)):
    return lax.broadcasted_iota(jnp.int32, shape, len(shape) - 2)


def split_parts(x):
    high = x.astype(BF16).astype(F32)
    rest = x - high
    middle = rest.astype(BF16).astype(F32)
    return high, middle, rest - middle


def block_transpose(a, b, c, d):
    lane = lanes()
    half = lane < 64
    even = (lane & 32) == 0
    a, c = jnp.where(half, a, pltpu.roll(c, 64, 1)), jnp.where(half, pltpu.roll(a, 64, 1), c)
    b, d = jnp.where(half, b, pltpu.roll(d, 64, 1)), jnp.where(half, pltpu.roll(b, 64, 1), d)
    a, b = jnp.where(even, a, pltpu.roll(b, 32, 1)), jnp.where(even, pltpu.roll(a, 96, 1), b)
    c, d = jnp.where(even, c, pltpu.roll(d, 32, 1)), jnp.where(even, pltpu.roll(c, 96, 1), d)
    return a, b, c, d


def pack(tiles, store, base):
    for first in range(0, len(tiles) // 4, 8):
        rows = [block_transpose(*tiles[4 * k : 4 * k + 4]) for k in range(first, first + 8)]
        for quarter in range(4):
            turned = jnp.swapaxes(jnp.stack([four[quarter] for four in rows]), 0, 1)
            for g in range(8):
                store[quarter * 8 + g, base + first : base + first + 8, :] = turned[g]


def donor_kernel(
    prop_hbm,
    index_hbm,
    fringe_hbm,
    weight_hbm,
    state_hbm,
    thrust_hbm,
    out_ref,
    thrust_out,
    prop_ref,
    index_ref,
    fringe_ref,
    weight_ref,
    state_ref,
    thrust_ref,
    sems,
):
    copies = [
        pltpu.make_async_copy(source, target, sems.at[at])
        for at, (source, target) in enumerate(
            (
                (index_hbm, index_ref),
                (prop_hbm, prop_ref),
                (weight_hbm, weight_ref),
                (fringe_hbm, fringe_ref),
                (state_hbm, state_ref),
                (thrust_hbm, thrust_ref),
            )
        )
    ]
    for copy in copies:
        copy.start()
    for copy in copies:
        copy.wait()
    for v in range(VARS):
        thrust_out[v] = jnp.full((8, 128), thrust_ref[v], F32)
    place = lax.axis_index("girth")
    index = index_ref[...]
    cells = lax.broadcasted_iota(jnp.int32, (256, 128), 0)
    pick = jnp.where(cells == index, 1.0, 0.0).astype(BF16)
    values = jnp.zeros((VARS, 128), F32)
    for part in split_parts(prop_ref[...]):
        values = values + jnp.dot(part.astype(BF16), pick, preferred_element_type=F32)
    values = values * weight_ref[...]
    target = jnp.where(index >= 0, fringe_ref[...], -1).astype(F32)
    edges = [
        (
            state_ref[pl.ds(row * 56, VARS, stride=8), :],
            state_ref[pl.ds(row * 56 + 7, VARS, stride=8), :],
        )
        for row in range(2)
    ]
    upper = lax.rem(place + 1, GIRTHS)
    for peer in range(GIRTHS):
        start = peer * DONOR_ROWS
        out_ref[start : start + VARS, :] = values
        out_ref[start + VARS : start + 8, :] = target
        out_ref[start + 8 : start + 24, :] = jnp.zeros((16, 128), F32)
        for row, (first, last) in enumerate(edges):
            at = start + 8 + row * 8
            out_ref[at : at + VARS, :] = jnp.where(upper == peer, last, first)


def fringe_sums(landed_ref, place):
    sub, lane = sublanes(), lanes()
    row = lanes((1, 128))
    slot = row & 31
    left = {}
    right = []
    for group in range(4):
        entries = jnp.zeros((8, 128), F32)
        for quarter in range(4):
            sender = group * 4 + quarter
            shift = lax.rem(32 * quarter + 8 - 8 * place + 128, 128)
            rolled = pltpu.roll(landed_ref[sender * DONOR_ROWS : sender * DONOR_ROWS + 8, :], shift, 1)
            entries = jnp.where((lane >> 5) == quarter, rolled, entries)
        target = entries[7:8, :].astype(jnp.int32)
        live = target >= 0
        tall = target >> 7
        own = jnp.where(live & (slot >= 8) & (slot < 16), tall, -1)
        low = jnp.where(live & (slot < 8) & ((tall & 7) == 7), tall >> 3, -1)
        high = jnp.where(live & (slot >= 16) & (slot < 24) & ((tall & 7) == 0), tall >> 3, -1)
        onto = lax.broadcasted_iota(jnp.int32, (128, 128), 0)
        right.append(jnp.where(onto == (target & 127), 1.0, 0.0).astype(BF16))
        parts = split_parts(entries)
        for which, part in enumerate(parts):
            counted = 1.0 if which == 0 else 0.0
            marked = jnp.where(sub == 7, counted, part)
            rows = []
            for r in range(2):
                inside = own == sub + 8 * r
                for v in range(8):
                    rows.append(jnp.where(inside, marked[v : v + 1, :], 0.0))
            for side in (low, high):
                for r in range(2):
                    rows.append(jnp.where(side == r, marked, 0.0))
            left[which, group] = jnp.concatenate(rows, axis=0).astype(BF16)
    right = jnp.concatenate(right, axis=1)
    total = None
    for which in range(3):
        lhs = jnp.concatenate([left[which, group] for group in range(4)], axis=1)
        part = lax.dot_general(lhs, right, (((1,), (1,)), ((), ())), preferred_element_type=F32)
        total = part if total is None else total + part
    return total


def flow_kernel(
    landed_ref,
    state_ref,
    face_ref,
    disk_ref,
    diag_ref,
    thrust_ref,
    coupling_hbm,
    send_ref,
    current_ref,
    down_ref,
    up_ref,
    partial_ref,
    factor_ref,
    coupling_ref,
    sem,
):
    coupling_copy = pltpu.make_async_copy(coupling_hbm, coupling_ref, sem)
    coupling_copy.start()
    tiles = [
        diag_ref[r, i, j].astype(F32) for r in range(2) for i in range(VARS) for j in range(VARS)
    ]
    pack(tiles[2:], send_ref, 8)
    place = lax.axis_index("girth")
    sub, lane = sublanes(), lanes()
    sums = fringe_sums(landed_ref, place)
    edges = []
    for side, peer in enumerate((lax.rem(place + 15, GIRTHS), lax.rem(place + 1, GIRTHS))):
        both = []
        for r in range(2):
            start = pl.multiple_of(peer * DONOR_ROWS + 8 + 8 * r, 8)
            edge = landed_ref[pl.ds(start, 8), :]
            found = sums[128 + side * 16 + r * 8 : 136 + side * 16 + r * 8, :]
            both.append(jnp.where(found[7:8, :] > 0.5, found, edge))
        edges.append(both)
    current, fringe = [], []
    for r in range(2):
        block = sums[r * 64 : (r + 1) * 64, :]
        hit = block[56:64, :] > 0.5
        fringe.append(hit)
        current.append(
            [jnp.where(hit, block[v * 8 : v * 8 + 8, :], state_ref[r, v]) for v in range(VARS)]
        )
    zero = jnp.zeros((8, 128), F32)
    residual = []
    for r in range(2):
        disk = disk_ref[r].astype(F32)
        residual.append([disk * thrust_ref[i] for i in range(VARS)])
    coupling_copy.wait()
    for direction in range(6):
        jumps = []
        for r in range(2):
            own = current[r]
            if direction < 2:
                beside = [zero] * VARS if direction == r else current[1 - r]
            elif direction == 2:
                beside = [
                    jnp.where(sub == 0, edges[0][r][v : v + 1, :], pltpu.roll(own[v], 1, 0))
                    for v in range(VARS)
                ]
            elif direction == 3:
                beside = [
                    jnp.where(sub == 7, edges[1][r][v : v + 1, :], pltpu.roll(own[v], 7, 0))
                    for v in range(VARS)
                ]
            elif direction == 4:
                beside = [jnp.where(lane == 0, 0.0, pltpu.roll(own[v], 1, 1)) for v in range(VARS)]
            else:
                beside = [
                    jnp.where(lane == 127, 0.0, pltpu.roll(own[v], 127, 1)) for v in range(VARS)
                ]
            factor = face_ref[r, direction]
            jumps.append([factor * (beside[v] - own[v]) for v in range(VARS)])
        for i in range(VARS):
            for j in range(VARS):
                weight = coupling_ref[direction, i, j]
                for r in range(2):
                    residual[r][i] = residual[r][i] + weight * jumps[r][j]
    factors = [face_ref[r, r] for r in range(2)]
    passed = []
    for r, ref in enumerate((down_ref, up_ref)):
        passed += [
            total_of([coupling_ref[r, i, j] * current[1 - r][j] for j in range(VARS)])
            for i in range(VARS)
        ]
        factor_ref[r] = factors[r]
        for v in range(VARS):
            ref[v] = passed[r * VARS + v]
            current_ref[r, v] = current[r][v]
            partial_ref[r, v] = residual[r][v]
    flow = [jnp.where(fringe[r], 0.0, x) for r in range(2) for x in residual[r]]
    flow += passed
    flow += [jnp.where(fringe[r], 0.0, factors[r]) for r in range(2)]
    flow += [diag_ref[0, 0, j].astype(F32) for j in range(2)]
    pack(flow, send_ref, 0)


def from_before(x, count):
    sub, lane = sublanes(), lanes()
    wrapped = jnp.where(lane < 32, 0.0, pltpu.roll(x, 32, 1))
    if count == 8:
        return wrapped
    return jnp.where(sub < count, pltpu.roll(wrapped, count, 0), pltpu.roll(x, count, 0))


def from_after(x, count):
    sub, lane = sublanes(), lanes()
    wrapped = jnp.where(lane >= 96, 0.0, pltpu.roll(x, 96, 1))
    if count == 8:
        return wrapped
    return jnp.where(
        sub >= 8 - count, pltpu.roll(wrapped, 8 - count, 0), pltpu.roll(x, 8 - count, 0)
    )


def total_of(terms):
    while len(terms) > 1:
        terms = [sum(terms[at : at + 2]) for at in range(0, len(terms), 2)]
    return terms[0]


def apply(ref, vector, add=None):
    result = []
    for i in range(VARS):
        terms = [ref[i * VARS + j] * vector[j] for j in range(VARS)]
        result.append(total_of(terms + ([add[i]] if add is not None else [])))
    return result


def spread_kernel(lower_ref, upper_ref, out_ref):
    for which, ref in enumerate((lower_ref, upper_ref)):
        for i in range(VARS):
            for j in range(VARS):
                out_ref[which, i * VARS + j] = jnp.full((8, 128), ref[i, j], F32)


def solve_kernel(
    moved_ref, spread_ref, back_ref, diag, near, far, maps, moved_maps
):
    flow = []
    for first in range(0, SEND_ROWS, 8):
        tiles = []
        for quarter in range(4):
            loaded = [moved_ref[quarter * 8 + s, first : first + 8, :] for s in range(8)]
            tiles.append(jnp.swapaxes(jnp.stack(loaded), 0, 1))
        for k in range(8):
            for at, tile in enumerate(block_transpose(*[four[k] for four in tiles])):
                place = 4 * (first + k) + at - 30
                if place < 0:
                    flow.append(tile)
                else:
                    diag[place // 49, place % 49] = tile
    beside = [
        [from_before(flow[14 + v], 1) for v in range(VARS)],
        [from_after(flow[21 + v], 1) for v in range(VARS)],
    ]
    source = [
        [-flow[r * VARS + i] - flow[28 + r] * beside[r][i] for i in range(VARS)] for r in range(2)
    ]

    def times(which, out):
        for k in range(VARS):
            column = [spread_ref[which, j * VARS + k] for j in range(VARS)]
            for r in range(2):
                for i in range(VARS):
                    out[r, i * VARS + k] = total_of(
                        [diag[r, i * VARS + j] * column[j] for j in range(VARS)]
                    )

    def multiply(a, b, out):
        for i in range(VARS):
            row = [a[i * VARS + j] for j in range(VARS)]
            for k in range(VARS):
                out[i * VARS + k] = total_of([row[j] * b[j * VARS + k] for j in range(VARS)])

    def scan(offset, shifted):
        for level, count in enumerate((1, 2, 4)):
            a = maps.at[level]
            for at in range(49):
                moved_maps[at] = shifted(a[at], count)
            offset = apply(a, [shifted(x, count) for x in offset], offset)
            multiply(a, moved_maps, maps.at[level + 1])
        a = maps.at[3]
        x = offset
        for _ in range(3):
            x = apply(a, [shifted(part, 8) for part in x], offset)
        return x

    times(0, near)
    times(1, far)
    first = apply(diag.at[0], source[0])
    second = apply(near.at[1], first, apply(diag.at[1], source[1]))
    multiply(near.at[1], near.at[0], maps.at[0])
    second = scan(second, from_before)
    first = apply(near.at[0], [from_before(x, 1) for x in second], first)
    multiply(far.at[0], far.at[1], maps.at[0])
    update_first = scan(apply(far.at[0], second, first), from_after)
    update_second = apply(far.at[1], [from_after(x, 1) for x in update_first], second)

    results = update_first + update_second + [jnp.zeros((8, 128), F32)] * 2
    for k in range(BACK_ROWS):
        for quarter, tile in enumerate(block_transpose(*results[4 * k : 4 * k + 4])):
            back_ref[pl.ds(quarter * 8 * BACK_ROWS + k, 8, stride=BACK_ROWS), :] = tile


def finish_kernel(
    returned_ref, current_ref, partial_ref, factor_ref, low_ref, high_ref, state_ref, residual_ref
):
    results = []
    for k in range(BACK_ROWS):
        results += block_transpose(
            *[
                returned_ref[pl.ds(quarter * 8 * BACK_ROWS + k, 8, stride=BACK_ROWS), :]
                for quarter in range(4)
            ]
        )
    for r, ref in enumerate((low_ref, high_ref)):
        for v in range(VARS):
            state_ref[r, v] = current_ref[r, v] + results[r * VARS + v]
            residual_ref[r, v] = partial_ref[r, v] + factor_ref[r] * ref[v]


VMEM = pl.BlockSpec(memory_space=pltpu.VMEM)
SMEM = pl.BlockSpec(memory_space=pltpu.SMEM)
HBM = pl.BlockSpec(memory_space=pltpu.HBM)


def exchange(block, axis, parts):
    rows = block.shape[0] // parts
    shaped = block.reshape(parts, rows, 128)
    return lax.all_to_all(shaped, axis, 0, 0, tiled=True).reshape(block.shape)


def per_device(
    state,
    propeller,
    donor_index,
    fringe_index,
    donor_weight,
    disk_mask,
    thrust,
    face,
    coupling,
    diag_inverse,
    lower_jacobian,
    upper_jacobian,
):
    inputs = (propeller, donor_index, fringe_index, donor_weight, state.reshape(112, 128), thrust)
    inputs = [pltpu.with_memory_space_constraint(x, pltpu.HBM) for x in inputs]
    donors, thrusts = pl.pallas_call(
        donor_kernel,
        out_shape=(
            jax.ShapeDtypeStruct((GIRTHS * DONOR_ROWS, 128), F32),
            jax.ShapeDtypeStruct((VARS, 8, 128), F32),
        ),
        in_specs=[HBM] * 6,
        out_specs=(VMEM, VMEM),
        scratch_shapes=[
            pltpu.VMEM((VARS, 256), F32),
            pltpu.VMEM((1, 128), jnp.int32),
            pltpu.VMEM((1, 128), jnp.int32),
            pltpu.VMEM((1, 128), F32),
            pltpu.VMEM((112, 128), F32),
            pltpu.SMEM((VARS,), F32),
            pltpu.SemaphoreType.DMA((6,)),
        ],
        compiler_params=pltpu.CompilerParams(vmem_limit_bytes=4 << 20),
        name="donors",
    )(*inputs)
    landed = exchange(donors, "girth", GIRTHS)
    row = jax.ShapeDtypeStruct(state.shape[1:], F32)
    both = jax.ShapeDtypeStruct(state.shape, F32)
    send, current, down, up, partial, factor = pl.pallas_call(
        flow_kernel,
        out_shape=(
            jax.ShapeDtypeStruct((STREAMS, SEND_ROWS, 128), F32),
            both,
            row,
            row,
            both,
            jax.ShapeDtypeStruct((2, 8, 128), F32),
        ),
        in_specs=[VMEM] * 6 + [pl.BlockSpec(memory_space=pl.ANY)],
        out_specs=(VMEM,) * 6,
        scratch_shapes=[pltpu.SMEM((6, VARS, VARS), F32), pltpu.SemaphoreType.DMA(())],
        compiler_params=pltpu.CompilerParams(vmem_limit_bytes=16 << 20),
        name="flow",
    )(landed, state, face, disk_mask, diag_inverse, thrusts, coupling)
    moved = lax.all_to_all(send, "stream", 0, 0, tiled=True)
    ahead = [(at, at + 1) for at in range(STREAMS - 1)]
    low = lax.ppermute(down, "stream", ahead)
    high = lax.ppermute(up, "stream", [(b, a) for a, b in ahead])
    lower, upper, _ = lax.optimization_barrier((lower_jacobian, upper_jacobian, factor))
    spread = pl.pallas_call(
        spread_kernel,
        out_shape=jax.ShapeDtypeStruct((2, VARS * VARS, 8, 128), F32),
        in_specs=[SMEM] * 2,
        out_specs=VMEM,
        compiler_params=pltpu.CompilerParams(vmem_limit_bytes=4 << 20),
        name="spread",
    )(lower, upper)
    back = pl.pallas_call(
        solve_kernel,
        out_shape=jax.ShapeDtypeStruct((STREAMS * BACK_ROWS, 128), F32),
        in_specs=[VMEM] * 2,
        out_specs=VMEM,
        scratch_shapes=[
            pltpu.VMEM((2, 49, 8, 128), F32),
            pltpu.VMEM((2, 49, 8, 128), F32),
            pltpu.VMEM((2, 49, 8, 128), F32),
            pltpu.VMEM((4, 49, 8, 128), F32),
            pltpu.VMEM((49, 8, 128), F32),
        ],
        compiler_params=pltpu.CompilerParams(vmem_limit_bytes=16 << 20),
        name="solve",
    )(moved, spread)
    back, low, high = lax.optimization_barrier((back, low, high))
    returned = exchange(back, "stream", STREAMS)
    return pl.pallas_call(
        finish_kernel,
        out_shape=(both, both),
        in_specs=[VMEM] * 6,
        out_specs=(VMEM, VMEM),
        compiler_params=pltpu.CompilerParams(vmem_limit_bytes=4 << 20),
        name="finish",
    )(returned, current, partial, factor, low, high)


def solution(mesh):
    placed = (
        P("stream", None, "girth", None),
        P(None, ("stream", "girth")),
        P(("stream", "girth"), None),
        P(("stream", "girth"), None),
        P(("stream", "girth"), None),
        P("stream", "girth", None),
        P(),
        P("stream", None, "girth", None),
        P(),
        P("stream", None, None, "girth", None),
        P(),
        P(),
    )
    return jax.shard_map(
        per_device,
        mesh=mesh,
        in_specs=placed,
        out_specs=(P("stream", None, "girth", None), P("stream", None, "girth", None)),
        check_vma=False,
    )
```

```python
import jax
import jax.numpy as jnp
from jax import lax
from jax.experimental import pallas as pl
from jax.experimental.pallas import tpu as pltpu
from jax.sharding import PartitionSpec as P

F32 = jnp.float32
BF16 = jnp.bfloat16
VARS = 7
STREAMS = 32
GIRTHS = 16
DONOR_ROWS = 24
SEND_ROWS = 32
BACK_ROWS = 4


def lanes(shape=(8, 128)):
    return lax.broadcasted_iota(jnp.int32, shape, len(shape) - 1)


def sublanes(shape=(8, 128)):
    return lax.broadcasted_iota(jnp.int32, shape, len(shape) - 2)


def split_parts(x):
    high = x.astype(BF16).astype(F32)
    rest = x - high
    middle = rest.astype(BF16).astype(F32)
    return high, middle, rest - middle


def block_transpose(a, b, c, d):
    lane = lanes()
    half = lane < 64
    even = (lane & 32) == 0
    a, c = jnp.where(half, a, pltpu.roll(c, 64, 1)), jnp.where(half, pltpu.roll(a, 64, 1), c)
    b, d = jnp.where(half, b, pltpu.roll(d, 64, 1)), jnp.where(half, pltpu.roll(b, 64, 1), d)
    a, b = jnp.where(even, a, pltpu.roll(b, 32, 1)), jnp.where(even, pltpu.roll(a, 96, 1), b)
    c, d = jnp.where(even, c, pltpu.roll(d, 32, 1)), jnp.where(even, pltpu.roll(c, 96, 1), d)
    return a, b, c, d


def pack(tiles, store, base):
    for first in range(0, len(tiles) // 4, 8):
        rows = [block_transpose(*tiles[4 * k : 4 * k + 4]) for k in range(first, first + 8)]
        for quarter in range(4):
            turned = jnp.swapaxes(jnp.stack([four[quarter] for four in rows]), 0, 1)
            for g in range(8):
                store[quarter * 8 + g, base + first : base + first + 8, :] = turned[g]


def donor_kernel(
    prop_hbm,
    index_hbm,
    fringe_hbm,
    weight_hbm,
    state_hbm,
    thrust_hbm,
    out_ref,
    thrust_out,
    prop_ref,
    index_ref,
    fringe_ref,
    weight_ref,
    state_ref,
    thrust_ref,
    sems,
):
    copies = [
        pltpu.make_async_copy(source, target, sems.at[at])
        for at, (source, target) in enumerate(
            (
                (index_hbm, index_ref),
                (prop_hbm, prop_ref),
                (weight_hbm, weight_ref),
                (fringe_hbm, fringe_ref),
                (state_hbm, state_ref),
                (thrust_hbm, thrust_ref),
            )
        )
    ]
    for copy in copies:
        copy.start()
    place = lax.axis_index("girth")
    for copy in copies[:2]:
        copy.wait()
    index = index_ref[...]
    cells = lax.broadcasted_iota(jnp.int32, (256, 128), 0)
    pick = jnp.where(cells == index, 1.0, 0.0).astype(BF16)
    values = jnp.zeros((VARS, 128), F32)
    for part in split_parts(prop_ref[...]):
        values = values + jnp.dot(part.astype(BF16), pick, preferred_element_type=F32)
    for copy in copies[2:]:
        copy.wait()
    values = values * weight_ref[...]
    target = jnp.where(index >= 0, fringe_ref[...], -1).astype(F32)
    edges = [
        (
            state_ref[pl.ds(row * 56, VARS, stride=8), :],
            state_ref[pl.ds(row * 56 + 7, VARS, stride=8), :],
        )
        for row in range(2)
    ]
    for v in range(VARS):
        thrust_out[v] = jnp.full((8, 128), thrust_ref[v], F32)
    upper = lax.rem(place + 1, GIRTHS)
    for peer in range(GIRTHS):
        start = peer * DONOR_ROWS
        out_ref[start : start + VARS, :] = values
        out_ref[start + VARS : start + 8, :] = target
        out_ref[start + 8 : start + 24, :] = jnp.zeros((16, 128), F32)
        for row, (first, last) in enumerate(edges):
            at = start + 8 + row * 8
            out_ref[at : at + VARS, :] = jnp.where(upper == peer, last, first)


def fringe_sums(landed_ref, place):
    sub, lane = sublanes(), lanes()
    row = lanes((1, 128))
    slot = row & 31
    left = {}
    right = []
    for group in range(4):
        entries = jnp.zeros((8, 128), F32)
        for quarter in range(4):
            sender = group * 4 + quarter
            shift = lax.rem(32 * quarter + 8 - 8 * place + 128, 128)
            rolled = pltpu.roll(landed_ref[sender * DONOR_ROWS : sender * DONOR_ROWS + 8, :], shift, 1)
            entries = jnp.where((lane >> 5) == quarter, rolled, entries)
        target = entries[7:8, :].astype(jnp.int32)
        live = target >= 0
        tall = target >> 7
        own = jnp.where(live & (slot >= 8) & (slot < 16), tall, -1)
        low = jnp.where(live & (slot < 8) & ((tall & 7) == 7), tall >> 3, -1)
        high = jnp.where(live & (slot >= 16) & (slot < 24) & ((tall & 7) == 0), tall >> 3, -1)
        onto = lax.broadcasted_iota(jnp.int32, (128, 128), 0)
        right.append(jnp.where(onto == (target & 127), 1.0, 0.0).astype(BF16))
        parts = split_parts(entries)
        for which, part in enumerate(parts):
            counted = 1.0 if which == 0 else 0.0
            marked = jnp.where(sub == 7, counted, part)
            rows = []
            for r in range(2):
                inside = own == sub + 8 * r
                for v in range(8):
                    rows.append(jnp.where(inside, marked[v : v + 1, :], 0.0))
            for side in (low, high):
                for r in range(2):
                    rows.append(jnp.where(side == r, marked, 0.0))
            left[which, group] = jnp.concatenate(rows, axis=0).astype(BF16)
    right = jnp.concatenate(right, axis=1)
    total = None
    for which in range(3):
        lhs = jnp.concatenate([left[which, group] for group in range(4)], axis=1)
        part = lax.dot_general(lhs, right, (((1,), (1,)), ((), ())), preferred_element_type=F32)
        total = part if total is None else total + part
    return total


def flow_kernel(
    landed_ref,
    state_ref,
    face_ref,
    disk_ref,
    diag_ref,
    thrust_ref,
    coupling_hbm,
    send_ref,
    current_ref,
    down_ref,
    up_ref,
    partial_ref,
    factor_ref,
    coupling_ref,
    sem,
):
    coupling_copy = pltpu.make_async_copy(coupling_hbm, coupling_ref, sem)
    coupling_copy.start()
    tiles = [
        diag_ref[r, i, j].astype(F32) for r in range(2) for i in range(VARS) for j in range(VARS)
    ]
    pack(tiles[2:], send_ref, 8)
    place = lax.axis_index("girth")
    sub, lane = sublanes(), lanes()
    sums = fringe_sums(landed_ref, place)
    edges = []
    for side, peer in enumerate((lax.rem(place + 15, GIRTHS), lax.rem(place + 1, GIRTHS))):
        both = []
        for r in range(2):
            start = pl.multiple_of(peer * DONOR_ROWS + 8 + 8 * r, 8)
            edge = landed_ref[pl.ds(start, 8), :]
            found = sums[128 + side * 16 + r * 8 : 136 + side * 16 + r * 8, :]
            both.append(jnp.where(found[7:8, :] > 0.5, found, edge))
        edges.append(both)
    current, fringe = [], []
    for r in range(2):
        block = sums[r * 64 : (r + 1) * 64, :]
        hit = block[56:64, :] > 0.5
        fringe.append(hit)
        current.append(
            [jnp.where(hit, block[v * 8 : v * 8 + 8, :], state_ref[r, v]) for v in range(VARS)]
        )
    zero = jnp.zeros((8, 128), F32)
    residual = []
    for r in range(2):
        disk = disk_ref[r].astype(F32)
        residual.append([disk * thrust_ref[i] for i in range(VARS)])
    coupling_copy.wait()
    for direction in range(6):
        jumps = []
        for r in range(2):
            own = current[r]
            if direction < 2:
                beside = [zero] * VARS if direction == r else current[1 - r]
            elif direction == 2:
                beside = [
                    jnp.where(sub == 0, edges[0][r][v : v + 1, :], pltpu.roll(own[v], 1, 0))
                    for v in range(VARS)
                ]
            elif direction == 3:
                beside = [
                    jnp.where(sub == 7, edges[1][r][v : v + 1, :], pltpu.roll(own[v], 7, 0))
                    for v in range(VARS)
                ]
            elif direction == 4:
                beside = [jnp.where(lane == 0, 0.0, pltpu.roll(own[v], 1, 1)) for v in range(VARS)]
            else:
                beside = [
                    jnp.where(lane == 127, 0.0, pltpu.roll(own[v], 127, 1)) for v in range(VARS)
                ]
            factor = face_ref[r, direction]
            jumps.append([factor * (beside[v] - own[v]) for v in range(VARS)])
        for i in range(VARS):
            for j in range(VARS):
                weight = coupling_ref[direction, i, j]
                for r in range(2):
                    residual[r][i] = residual[r][i] + weight * jumps[r][j]
    factors = [face_ref[r, r] for r in range(2)]
    passed = []
    for r, ref in enumerate((down_ref, up_ref)):
        passed += [
            total_of([coupling_ref[r, i, j] * current[1 - r][j] for j in range(VARS)])
            for i in range(VARS)
        ]
        factor_ref[r] = factors[r]
        for v in range(VARS):
            ref[v] = passed[r * VARS + v]
            current_ref[r, v] = current[r][v]
            partial_ref[r, v] = residual[r][v]
    flow = [jnp.where(fringe[r], 0.0, x) for r in range(2) for x in residual[r]]
    flow += passed
    flow += [jnp.where(fringe[r], 0.0, factors[r]) for r in range(2)]
    flow += [diag_ref[0, 0, j].astype(F32) for j in range(2)]
    pack(flow, send_ref, 0)


def from_before(x):
    sub, lane = sublanes(), lanes()
    wrapped = jnp.where(lane < 32, 0.0, pltpu.roll(x, 32, 1))
    return jnp.where(sub < 1, pltpu.roll(wrapped, 1, 0), pltpu.roll(x, 1, 0))


def from_after(x):
    sub, lane = sublanes(), lanes()
    wrapped = jnp.where(lane >= 96, 0.0, pltpu.roll(x, 96, 1))
    return jnp.where(sub >= 7, pltpu.roll(wrapped, 7, 0), pltpu.roll(x, 7, 0))


def within_before(x, count, fill=0.0):
    return jnp.where(sublanes() < count, fill, pltpu.roll(x, count, 0))


def within_after(x, count, fill=0.0):
    return jnp.where(sublanes() >= 8 - count, fill, pltpu.roll(x, 8 - count, 0))


def eight_before(x):
    x = jnp.where(lanes() < 32, 0.0, pltpu.roll(x, 32, 1))
    return jnp.broadcast_to(x[7:8, :], (8, 128))


def eight_after(x):
    x = jnp.where(lanes() >= 96, 0.0, pltpu.roll(x, 96, 1))
    return jnp.broadcast_to(x[0:1, :], (8, 128))


def total_of(terms):
    total = terms[0]
    for term in terms[1:]:
        total = total + term
    return total


def apply(ref, vector, add=None):
    result = []
    for i in range(VARS):
        terms = [ref[i * VARS + j] * vector[j] for j in range(VARS)]
        result.append(total_of(terms + ([add[i]] if add is not None else [])))
    return result


def spread_kernel(lower_ref, upper_ref, out_ref):
    for which, ref in enumerate((lower_ref, upper_ref)):
        for i in range(VARS):
            for j in range(VARS):
                out_ref[which, i * VARS + j] = jnp.full((8, 128), ref[i, j], F32)


def solve_kernel(
    moved_ref, spread_ref, back_ref, diag, near, far, maps, moved_maps
):
    flow = []
    for first in range(0, SEND_ROWS, 8):
        tiles = []
        for quarter in range(4):
            loaded = [moved_ref[quarter * 8 + s, first : first + 8, :] for s in range(8)]
            tiles.append(jnp.swapaxes(jnp.stack(loaded), 0, 1))
        for k in range(8):
            for at, tile in enumerate(block_transpose(*[four[k] for four in tiles])):
                place = 4 * (first + k) + at - 30
                if place < 0:
                    flow.append(tile)
                else:
                    diag[place // 49, place % 49] = tile
    beside = [
        [from_before(flow[14 + v]) for v in range(VARS)],
        [from_after(flow[21 + v]) for v in range(VARS)],
    ]
    source = [
        [-flow[r * VARS + i] - flow[28 + r] * beside[r][i] for i in range(VARS)] for r in range(2)
    ]

    def times(which, out):
        for k in range(VARS):
            column = [spread_ref[which, j * VARS + k] for j in range(VARS)]
            for r in range(2):
                for i in range(VARS):
                    out[r, i * VARS + k] = total_of(
                        [diag[r, i * VARS + j] * column[j] for j in range(VARS)]
                    )

    def multiply(a, b, out):
        for i in range(VARS):
            row = [a[i * VARS + j] for j in range(VARS)]
            for k in range(VARS):
                out[i * VARS + k] = total_of([row[j] * b[j * VARS + k] for j in range(VARS)])

    def scan(offset, within, eight):
        for level, count in enumerate((1, 2, 4)):
            a = maps.at[level]
            for at in range(49):
                moved_maps[at] = within(a[at], count, float(at // VARS == at % VARS))
            offset = apply(a, [within(x, count) for x in offset], offset)
            multiply(a, moved_maps, maps.at[level + 1])
        a = maps.at[3]
        x = offset
        for _ in range(3):
            x = apply(a, [eight(part) for part in x], offset)
        return x

    times(0, near)
    times(1, far)
    first = apply(diag.at[0], source[0])
    second = apply(near.at[1], first, apply(diag.at[1], source[1]))
    multiply(near.at[1], near.at[0], maps.at[0])
    second = scan(second, within_before, eight_before)
    first = apply(near.at[0], [from_before(x) for x in second], first)
    multiply(far.at[0], far.at[1], maps.at[0])
    update_first = scan(apply(far.at[0], second, first), within_after, eight_after)
    update_second = apply(far.at[1], [from_after(x) for x in update_first], second)

    results = update_first + update_second + [jnp.zeros((8, 128), F32)] * 2
    for k in range(BACK_ROWS):
        for quarter, tile in enumerate(block_transpose(*results[4 * k : 4 * k + 4])):
            back_ref[pl.ds(quarter * 8 * BACK_ROWS + k, 8, stride=BACK_ROWS), :] = tile


def finish_kernel(
    returned_ref, current_ref, partial_ref, factor_ref, low_ref, high_ref, state_ref, residual_ref
):
    results = []
    for k in range(BACK_ROWS):
        results += block_transpose(
            *[
                returned_ref[pl.ds(quarter * 8 * BACK_ROWS + k, 8, stride=BACK_ROWS), :]
                for quarter in range(4)
            ]
        )
    for r, ref in enumerate((low_ref, high_ref)):
        for v in range(VARS):
            state_ref[r, v] = current_ref[r, v] + results[r * VARS + v]
            residual_ref[r, v] = partial_ref[r, v] + factor_ref[r] * ref[v]


VMEM = pl.BlockSpec(memory_space=pltpu.VMEM)
SMEM = pl.BlockSpec(memory_space=pltpu.SMEM)
HBM = pl.BlockSpec(memory_space=pltpu.HBM)


def exchange(block, axis, parts):
    rows = block.shape[0] // parts
    shaped = block.reshape(parts, rows, 128)
    return lax.all_to_all(shaped, axis, 0, 0, tiled=True).reshape(block.shape)


def per_device(
    state,
    propeller,
    donor_index,
    fringe_index,
    donor_weight,
    disk_mask,
    thrust,
    face,
    coupling,
    diag_inverse,
    lower_jacobian,
    upper_jacobian,
):
    inputs = (propeller, donor_index, fringe_index, donor_weight, state.reshape(112, 128), thrust)
    inputs = [pltpu.with_memory_space_constraint(x, pltpu.HBM) for x in inputs]
    donors, thrusts = pl.pallas_call(
        donor_kernel,
        out_shape=(
            jax.ShapeDtypeStruct((GIRTHS * DONOR_ROWS, 128), F32),
            jax.ShapeDtypeStruct((VARS, 8, 128), F32),
        ),
        in_specs=[HBM] * 6,
        out_specs=(VMEM, VMEM),
        scratch_shapes=[
            pltpu.VMEM((VARS, 256), F32),
            pltpu.VMEM((1, 128), jnp.int32),
            pltpu.VMEM((1, 128), jnp.int32),
            pltpu.VMEM((1, 128), F32),
            pltpu.VMEM((112, 128), F32),
            pltpu.SMEM((VARS,), F32),
            pltpu.SemaphoreType.DMA((6,)),
        ],
        compiler_params=pltpu.CompilerParams(vmem_limit_bytes=4 << 20),
        name="donors",
    )(*inputs)
    landed = exchange(donors, "girth", GIRTHS)
    row = jax.ShapeDtypeStruct(state.shape[1:], F32)
    both = jax.ShapeDtypeStruct(state.shape, F32)
    send, current, down, up, partial, factor = pl.pallas_call(
        flow_kernel,
        out_shape=(
            jax.ShapeDtypeStruct((STREAMS, SEND_ROWS, 128), F32),
            both,
            row,
            row,
            both,
            jax.ShapeDtypeStruct((2, 8, 128), F32),
        ),
        in_specs=[VMEM] * 6 + [pl.BlockSpec(memory_space=pl.ANY)],
        out_specs=(VMEM,) * 6,
        scratch_shapes=[pltpu.SMEM((6, VARS, VARS), F32), pltpu.SemaphoreType.DMA(())],
        compiler_params=pltpu.CompilerParams(vmem_limit_bytes=16 << 20),
        name="flow",
    )(landed, state, face, disk_mask, diag_inverse, thrusts, coupling)
    moved = lax.all_to_all(send, "stream", 0, 0, tiled=True)
    ahead = [(at, at + 1) for at in range(STREAMS - 1)]
    low = lax.ppermute(down, "stream", ahead)
    high = lax.ppermute(up, "stream", [(b, a) for a, b in ahead])
    lower, upper, _ = lax.optimization_barrier((lower_jacobian, upper_jacobian, factor))
    spread = pl.pallas_call(
        spread_kernel,
        out_shape=jax.ShapeDtypeStruct((2, VARS * VARS, 8, 128), F32),
        in_specs=[SMEM] * 2,
        out_specs=VMEM,
        compiler_params=pltpu.CompilerParams(vmem_limit_bytes=4 << 20),
        name="spread",
    )(lower, upper)
    back = pl.pallas_call(
        solve_kernel,
        out_shape=jax.ShapeDtypeStruct((STREAMS * BACK_ROWS, 128), F32),
        in_specs=[VMEM] * 2,
        out_specs=VMEM,
        scratch_shapes=[
            pltpu.VMEM((2, 49, 8, 128), F32),
            pltpu.VMEM((2, 49, 8, 128), F32),
            pltpu.VMEM((2, 49, 8, 128), F32),
            pltpu.VMEM((4, 49, 8, 128), F32),
            pltpu.VMEM((49, 8, 128), F32),
        ],
        compiler_params=pltpu.CompilerParams(vmem_limit_bytes=16 << 20),
        name="solve",
    )(moved, spread)
    back, low, high = lax.optimization_barrier((back, low, high))
    returned = exchange(back, "stream", STREAMS)
    return pl.pallas_call(
        finish_kernel,
        out_shape=(both, both),
        in_specs=[VMEM] * 6,
        out_specs=(VMEM, VMEM),
        compiler_params=pltpu.CompilerParams(vmem_limit_bytes=4 << 20),
        name="finish",
    )(returned, current, partial, factor, low, high)


def solution(mesh):
    placed = (
        P("stream", None, "girth", None),
        P(None, ("stream", "girth")),
        P(("stream", "girth"), None),
        P(("stream", "girth"), None),
        P(("stream", "girth"), None),
        P("stream", "girth", None),
        P(),
        P("stream", None, "girth", None),
        P(),
        P("stream", None, None, "girth", None),
        P(),
        P(),
    )
    return jax.shard_map(
        per_device,
        mesh=mesh,
        in_specs=placed,
        out_specs=(P("stream", None, "girth", None), P("stream", None, "girth", None)),
        check_vma=False,
    )
```

```python
import jax
import jax.numpy as jnp
from jax import lax
from jax.experimental import pallas as pl
from jax.experimental.pallas import tpu as pltpu
from jax.sharding import PartitionSpec as P

F32 = jnp.float32
BF16 = jnp.bfloat16
VARS = 7
STREAMS = 32
GIRTHS = 16
DONOR_ROWS = 24
SEND_ROWS = 32
BACK_ROWS = 4


def lanes(shape=(8, 128)):
    return lax.broadcasted_iota(jnp.int32, shape, len(shape) - 1)


def sublanes(shape=(8, 128)):
    return lax.broadcasted_iota(jnp.int32, shape, len(shape) - 2)


def split_parts(x):
    high = x.astype(BF16).astype(F32)
    rest = x - high
    middle = rest.astype(BF16).astype(F32)
    return high, middle, rest - middle


def block_transpose(a, b, c, d):
    lane = lanes()
    half = lane < 64
    even = (lane & 32) == 0
    a, c = jnp.where(half, a, pltpu.roll(c, 64, 1)), jnp.where(half, pltpu.roll(a, 64, 1), c)
    b, d = jnp.where(half, b, pltpu.roll(d, 64, 1)), jnp.where(half, pltpu.roll(b, 64, 1), d)
    a, b = jnp.where(even, a, pltpu.roll(b, 32, 1)), jnp.where(even, pltpu.roll(a, 96, 1), b)
    c, d = jnp.where(even, c, pltpu.roll(d, 32, 1)), jnp.where(even, pltpu.roll(c, 96, 1), d)
    return a, b, c, d


def pack(tiles, store, base):
    for first in range(0, len(tiles) // 4, 8):
        rows = [block_transpose(*tiles[4 * k : 4 * k + 4]) for k in range(first, first + 8)]
        for quarter in range(4):
            turned = jnp.swapaxes(jnp.stack([four[quarter] for four in rows]), 0, 1)
            for g in range(8):
                store[quarter * 8 + g, base + first : base + first + 8, :] = turned[g]


def donor_kernel(
    prop_hbm,
    index_hbm,
    fringe_hbm,
    weight_hbm,
    state_hbm,
    thrust_hbm,
    out_ref,
    thrust_out,
    prop_ref,
    index_ref,
    fringe_ref,
    weight_ref,
    state_ref,
    thrust_ref,
    sems,
):
    copies = [
        pltpu.make_async_copy(source, target, sems.at[at])
        for at, (source, target) in enumerate(
            (
                (index_hbm, index_ref),
                (prop_hbm, prop_ref),
                (weight_hbm, weight_ref),
                (fringe_hbm, fringe_ref),
                (state_hbm, state_ref),
                (thrust_hbm, thrust_ref),
            )
        )
    ]
    for copy in copies:
        copy.start()
    place = lax.axis_index("girth")
    for copy in copies[:2]:
        copy.wait()
    index = index_ref[...]
    cells = lax.broadcasted_iota(jnp.int32, (256, 128), 0)
    pick = jnp.where(cells == index, 1.0, 0.0).astype(BF16)
    values = jnp.zeros((VARS, 128), F32)
    for part in split_parts(prop_ref[...]):
        values = values + jnp.dot(part.astype(BF16), pick, preferred_element_type=F32)
    for copy in copies[2:]:
        copy.wait()
    values = values * weight_ref[...]
    target = jnp.where(index >= 0, fringe_ref[...], -1).astype(F32)
    edges = [
        (
            state_ref[pl.ds(row * 56, VARS, stride=8), :],
            state_ref[pl.ds(row * 56 + 7, VARS, stride=8), :],
        )
        for row in range(2)
    ]
    for v in range(VARS):
        thrust_out[v] = jnp.full((8, 128), thrust_ref[v], F32)
    upper = lax.rem(place + 1, GIRTHS)
    for peer in range(GIRTHS):
        start = peer * DONOR_ROWS
        out_ref[start : start + VARS, :] = values
        out_ref[start + VARS : start + 8, :] = target
        out_ref[start + 8 : start + 24, :] = jnp.zeros((16, 128), F32)
        for row, (first, last) in enumerate(edges):
            at = start + 8 + row * 8
            out_ref[at : at + VARS, :] = jnp.where(upper == peer, last, first)


def fringe_sums(landed_ref, place):
    sub, lane = sublanes(), lanes()
    row = lanes((1, 128))
    slot = row & 31
    left = {}
    right = []
    for group in range(4):
        entries = jnp.zeros((8, 128), F32)
        for quarter in range(4):
            sender = group * 4 + quarter
            shift = lax.rem(32 * quarter + 8 - 8 * place + 128, 128)
            rolled = pltpu.roll(landed_ref[sender * DONOR_ROWS : sender * DONOR_ROWS + 8, :], shift, 1)
            entries = jnp.where((lane >> 5) == quarter, rolled, entries)
        target = entries[7:8, :].astype(jnp.int32)
        live = target >= 0
        tall = target >> 7
        own = jnp.where(live & (slot >= 8) & (slot < 16), tall, -1)
        low = jnp.where(live & (slot < 8) & ((tall & 7) == 7), tall >> 3, -1)
        high = jnp.where(live & (slot >= 16) & (slot < 24) & ((tall & 7) == 0), tall >> 3, -1)
        onto = lax.broadcasted_iota(jnp.int32, (128, 128), 0)
        right.append(jnp.where(onto == (target & 127), 1.0, 0.0).astype(BF16))
        parts = split_parts(entries)
        for which, part in enumerate(parts):
            counted = 1.0 if which == 0 else 0.0
            marked = jnp.where(sub == 7, counted, part)
            rows = []
            for r in range(2):
                inside = own == sub + 8 * r
                for v in range(8):
                    rows.append(jnp.where(inside, marked[v : v + 1, :], 0.0))
            for side in (low, high):
                for r in range(2):
                    rows.append(jnp.where(side == r, marked, 0.0))
            left[which, group] = jnp.concatenate(rows, axis=0).astype(BF16)
    right = jnp.concatenate(right, axis=1)
    lhs = jnp.concatenate(
        [
            jnp.concatenate([left[which, group] for group in range(4)], axis=1)
            for which in range(3)
        ],
        axis=0,
    )
    sums = lax.dot_general(lhs, right, (((1,), (1,)), ((), ())), preferred_element_type=F32)
    return sums[0:160, :] + sums[160:320, :] + sums[320:480, :]


def flow_kernel(
    landed_ref,
    state_ref,
    face_ref,
    disk_ref,
    diag_ref,
    thrust_ref,
    coupling_hbm,
    send_ref,
    current_ref,
    down_ref,
    up_ref,
    partial_ref,
    factor_ref,
    coupling_ref,
    sem,
):
    coupling_copy = pltpu.make_async_copy(coupling_hbm, coupling_ref, sem)
    coupling_copy.start()
    tiles = [
        diag_ref[r, i, j].astype(F32) for r in range(2) for i in range(VARS) for j in range(VARS)
    ]
    pack(tiles[2:], send_ref, 8)
    place = lax.axis_index("girth")
    sub, lane = sublanes(), lanes()
    sums = fringe_sums(landed_ref, place)
    edges = []
    for side, peer in enumerate((lax.rem(place + 15, GIRTHS), lax.rem(place + 1, GIRTHS))):
        both = []
        for r in range(2):
            start = pl.multiple_of(peer * DONOR_ROWS + 8 + 8 * r, 8)
            edge = landed_ref[pl.ds(start, 8), :]
            found = sums[128 + side * 16 + r * 8 : 136 + side * 16 + r * 8, :]
            both.append(jnp.where(found[7:8, :] > 0.5, found, edge))
        edges.append(both)
    current, fringe = [], []
    for r in range(2):
        block = sums[r * 64 : (r + 1) * 64, :]
        hit = block[56:64, :] > 0.5
        fringe.append(hit)
        current.append(
            [jnp.where(hit, block[v * 8 : v * 8 + 8, :], state_ref[r, v]) for v in range(VARS)]
        )
    zero = jnp.zeros((8, 128), F32)
    residual = []
    for r in range(2):
        disk = disk_ref[r].astype(F32)
        residual.append([disk * thrust_ref[i] for i in range(VARS)])
    coupling_copy.wait()
    for direction in range(6):
        jumps = []
        for r in range(2):
            own = current[r]
            if direction < 2:
                beside = [zero] * VARS if direction == r else current[1 - r]
            elif direction == 2:
                beside = [
                    jnp.where(sub == 0, edges[0][r][v : v + 1, :], pltpu.roll(own[v], 1, 0))
                    for v in range(VARS)
                ]
            elif direction == 3:
                beside = [
                    jnp.where(sub == 7, edges[1][r][v : v + 1, :], pltpu.roll(own[v], 7, 0))
                    for v in range(VARS)
                ]
            elif direction == 4:
                beside = [jnp.where(lane == 0, 0.0, pltpu.roll(own[v], 1, 1)) for v in range(VARS)]
            else:
                beside = [
                    jnp.where(lane == 127, 0.0, pltpu.roll(own[v], 127, 1)) for v in range(VARS)
                ]
            factor = face_ref[r, direction]
            jumps.append([factor * (beside[v] - own[v]) for v in range(VARS)])
        for i in range(VARS):
            for j in range(VARS):
                weight = coupling_ref[direction, i, j]
                for r in range(2):
                    residual[r][i] = residual[r][i] + weight * jumps[r][j]
    factors = [face_ref[r, r] for r in range(2)]
    passed = []
    for r, ref in enumerate((down_ref, up_ref)):
        passed += [
            total_of([coupling_ref[r, i, j] * current[1 - r][j] for j in range(VARS)])
            for i in range(VARS)
        ]
        factor_ref[r] = factors[r]
        for v in range(VARS):
            ref[v] = passed[r * VARS + v]
            current_ref[r, v] = current[r][v]
            partial_ref[r, v] = residual[r][v]
    flow = [jnp.where(fringe[r], 0.0, x) for r in range(2) for x in residual[r]]
    flow += passed
    flow += [jnp.where(fringe[r], 0.0, factors[r]) for r in range(2)]
    flow += [diag_ref[0, 0, j].astype(F32) for j in range(2)]
    pack(flow, send_ref, 0)


def from_before(x):
    sub, lane = sublanes(), lanes()
    wrapped = jnp.where(lane < 32, 0.0, pltpu.roll(x, 32, 1))
    return jnp.where(sub < 1, pltpu.roll(wrapped, 1, 0), pltpu.roll(x, 1, 0))


def from_after(x):
    sub, lane = sublanes(), lanes()
    wrapped = jnp.where(lane >= 96, 0.0, pltpu.roll(x, 96, 1))
    return jnp.where(sub >= 7, pltpu.roll(wrapped, 7, 0), pltpu.roll(x, 7, 0))


def within_before(x, count, fill=0.0):
    return jnp.where(sublanes() < count, fill, pltpu.roll(x, count, 0))


def within_after(x, count, fill=0.0):
    return jnp.where(sublanes() >= 8 - count, fill, pltpu.roll(x, 8 - count, 0))


def eight_before(x):
    x = jnp.broadcast_to(x[7:8, :], (8, 128))
    return jnp.where(lanes() < 32, 0.0, pltpu.roll(x, 32, 1))


def eight_after(x):
    x = jnp.broadcast_to(x[0:1, :], (8, 128))
    return jnp.where(lanes() >= 96, 0.0, pltpu.roll(x, 96, 1))


def total_of(terms):
    total = terms[0]
    for term in terms[1:]:
        total = total + term
    return total


def apply(ref, vector, add=None):
    result = []
    for i in range(VARS):
        terms = [ref[i * VARS + j] * vector[j] for j in range(VARS)]
        result.append(total_of(terms + ([add[i]] if add is not None else [])))
    return result


def spread_kernel(lower_ref, upper_ref, out_ref):
    for which, ref in enumerate((lower_ref, upper_ref)):
        for i in range(VARS):
            for j in range(VARS):
                out_ref[which, i * VARS + j] = jnp.full((8, 128), ref[i, j], F32)


def solve_kernel(
    moved_ref, spread_ref, back_ref, diag, near, far, maps, moved_maps
):
    flow = []
    for first in range(0, SEND_ROWS, 8):
        tiles = []
        for quarter in range(4):
            loaded = [moved_ref[quarter * 8 + s, first : first + 8, :] for s in range(8)]
            tiles.append(jnp.swapaxes(jnp.stack(loaded), 0, 1))
        for k in range(8):
            for at, tile in enumerate(block_transpose(*[four[k] for four in tiles])):
                place = 4 * (first + k) + at - 30
                if place < 0:
                    flow.append(tile)
                else:
                    diag[place // 49, place % 49] = tile
    beside = [
        [from_before(flow[14 + v]) for v in range(VARS)],
        [from_after(flow[21 + v]) for v in range(VARS)],
    ]
    source = [
        [-flow[r * VARS + i] - flow[28 + r] * beside[r][i] for i in range(VARS)] for r in range(2)
    ]

    def times(which, out):
        for k in range(VARS):
            column = [spread_ref[which, j * VARS + k] for j in range(VARS)]
            for r in range(2):
                for i in range(VARS):
                    out[r, i * VARS + k] = total_of(
                        [diag[r, i * VARS + j] * column[j] for j in range(VARS)]
                    )

    def multiply(a, b, out):
        for i in range(VARS):
            row = [a[i * VARS + j] for j in range(VARS)]
            for k in range(VARS):
                out[i * VARS + k] = total_of([row[j] * b[j * VARS + k] for j in range(VARS)])

    def scan(offset, within, eight):
        for level, count in enumerate((1, 2, 4)):
            a = maps.at[level]
            for at in range(49):
                moved_maps[at] = within(a[at], count, float(at // VARS == at % VARS))
            offset = apply(a, [within(x, count) for x in offset], offset)
            multiply(a, moved_maps, maps.at[level + 1])
        a = maps.at[3]
        x = offset
        for _ in range(3):
            x = apply(a, [eight(part) for part in x], offset)
        return x

    times(0, near)
    times(1, far)
    first = apply(diag.at[0], source[0])
    second = apply(near.at[1], first, apply(diag.at[1], source[1]))
    multiply(near.at[1], near.at[0], maps.at[0])
    second = scan(second, within_before, eight_before)
    first = apply(near.at[0], [from_before(x) for x in second], first)
    multiply(far.at[0], far.at[1], maps.at[0])
    update_first = scan(apply(far.at[0], second, first), within_after, eight_after)
    update_second = apply(far.at[1], [from_after(x) for x in update_first], second)

    results = update_first + update_second + [jnp.zeros((8, 128), F32)] * 2
    for k in range(BACK_ROWS):
        for quarter, tile in enumerate(block_transpose(*results[4 * k : 4 * k + 4])):
            back_ref[pl.ds(quarter * 8 * BACK_ROWS + k, 8, stride=BACK_ROWS), :] = tile


def finish_kernel(
    returned_ref, current_ref, partial_ref, factor_ref, low_ref, high_ref, state_ref, residual_ref
):
    results = []
    for k in range(BACK_ROWS):
        results += block_transpose(
            *[
                returned_ref[pl.ds(quarter * 8 * BACK_ROWS + k, 8, stride=BACK_ROWS), :]
                for quarter in range(4)
            ]
        )
    for r, ref in enumerate((low_ref, high_ref)):
        for v in range(VARS):
            state_ref[r, v] = current_ref[r, v] + results[r * VARS + v]
            residual_ref[r, v] = partial_ref[r, v] + factor_ref[r] * ref[v]


VMEM = pl.BlockSpec(memory_space=pltpu.VMEM)
SMEM = pl.BlockSpec(memory_space=pltpu.SMEM)
HBM = pl.BlockSpec(memory_space=pltpu.HBM)


def exchange(block, axis, parts):
    rows = block.shape[0] // parts
    shaped = block.reshape(parts, rows, 128)
    return lax.all_to_all(shaped, axis, 0, 0, tiled=True).reshape(block.shape)


def per_device(
    state,
    propeller,
    donor_index,
    fringe_index,
    donor_weight,
    disk_mask,
    thrust,
    face,
    coupling,
    diag_inverse,
    lower_jacobian,
    upper_jacobian,
):
    inputs = (propeller, donor_index, fringe_index, donor_weight, state.reshape(112, 128), thrust)
    inputs = [pltpu.with_memory_space_constraint(x, pltpu.HBM) for x in inputs]
    donors, thrusts = pl.pallas_call(
        donor_kernel,
        out_shape=(
            jax.ShapeDtypeStruct((GIRTHS * DONOR_ROWS, 128), F32),
            jax.ShapeDtypeStruct((VARS, 8, 128), F32),
        ),
        in_specs=[HBM] * 6,
        out_specs=(VMEM, VMEM),
        scratch_shapes=[
            pltpu.VMEM((VARS, 256), F32),
            pltpu.VMEM((1, 128), jnp.int32),
            pltpu.VMEM((1, 128), jnp.int32),
            pltpu.VMEM((1, 128), F32),
            pltpu.VMEM((112, 128), F32),
            pltpu.SMEM((VARS,), F32),
            pltpu.SemaphoreType.DMA((6,)),
        ],
        compiler_params=pltpu.CompilerParams(vmem_limit_bytes=4 << 20),
        name="donors",
    )(*inputs)
    landed = exchange(donors, "girth", GIRTHS)
    row = jax.ShapeDtypeStruct(state.shape[1:], F32)
    both = jax.ShapeDtypeStruct(state.shape, F32)
    send, current, down, up, partial, factor = pl.pallas_call(
        flow_kernel,
        out_shape=(
            jax.ShapeDtypeStruct((STREAMS, SEND_ROWS, 128), F32),
            both,
            row,
            row,
            both,
            jax.ShapeDtypeStruct((2, 8, 128), F32),
        ),
        in_specs=[VMEM] * 6 + [pl.BlockSpec(memory_space=pl.ANY)],
        out_specs=(VMEM,) * 6,
        scratch_shapes=[pltpu.SMEM((6, VARS, VARS), F32), pltpu.SemaphoreType.DMA(())],
        compiler_params=pltpu.CompilerParams(vmem_limit_bytes=16 << 20),
        name="flow",
    )(landed, state, face, disk_mask, diag_inverse, thrusts, coupling)
    moved = lax.all_to_all(send, "stream", 0, 0, tiled=True)
    ahead = [(at, at + 1) for at in range(STREAMS - 1)]
    low = lax.ppermute(down, "stream", ahead)
    high = lax.ppermute(up, "stream", [(b, a) for a, b in ahead])
    lower, upper, _ = lax.optimization_barrier((lower_jacobian, upper_jacobian, factor))
    spread = pl.pallas_call(
        spread_kernel,
        out_shape=jax.ShapeDtypeStruct((2, VARS * VARS, 8, 128), F32),
        in_specs=[SMEM] * 2,
        out_specs=VMEM,
        compiler_params=pltpu.CompilerParams(vmem_limit_bytes=4 << 20),
        name="spread",
    )(lower, upper)
    back = pl.pallas_call(
        solve_kernel,
        out_shape=jax.ShapeDtypeStruct((STREAMS * BACK_ROWS, 128), F32),
        in_specs=[VMEM] * 2,
        out_specs=VMEM,
        scratch_shapes=[
            pltpu.VMEM((2, 49, 8, 128), F32),
            pltpu.VMEM((2, 49, 8, 128), F32),
            pltpu.VMEM((2, 49, 8, 128), F32),
            pltpu.VMEM((4, 49, 8, 128), F32),
            pltpu.VMEM((49, 8, 128), F32),
        ],
        compiler_params=pltpu.CompilerParams(vmem_limit_bytes=16 << 20),
        name="solve",
    )(moved, spread)
    back, low, high = lax.optimization_barrier((back, low, high))
    returned = exchange(back, "stream", STREAMS)
    return pl.pallas_call(
        finish_kernel,
        out_shape=(both, both),
        in_specs=[VMEM] * 6,
        out_specs=(VMEM, VMEM),
        compiler_params=pltpu.CompilerParams(vmem_limit_bytes=4 << 20),
        name="finish",
    )(returned, current, partial, factor, low, high)


def solution(mesh):
    placed = (
        P("stream", None, "girth", None),
        P(None, ("stream", "girth")),
        P(("stream", "girth"), None),
        P(("stream", "girth"), None),
        P(("stream", "girth"), None),
        P("stream", "girth", None),
        P(),
        P("stream", None, "girth", None),
        P(),
        P("stream", None, None, "girth", None),
        P(),
        P(),
    )
    return jax.shard_map(
        per_device,
        mesh=mesh,
        in_specs=placed,
        out_specs=(P("stream", None, "girth", None), P("stream", None, "girth", None)),
        check_vma=False,
    )
```

```python
import jax
import jax.numpy as jnp
from jax import lax
from jax.experimental import pallas as pl
from jax.experimental.pallas import tpu as pltpu
from jax.sharding import PartitionSpec as P

F32 = jnp.float32
BF16 = jnp.bfloat16
VARS = 7
STREAMS = 32
GIRTHS = 16
DONOR_ROWS = 24
SEND_ROWS = 32
BACK_ROWS = 4


def lanes(shape=(8, 128)):
    return lax.broadcasted_iota(jnp.int32, shape, len(shape) - 1)


def sublanes(shape=(8, 128)):
    return lax.broadcasted_iota(jnp.int32, shape, len(shape) - 2)


def split_parts(x):
    high = x.astype(BF16).astype(F32)
    rest = x - high
    middle = rest.astype(BF16).astype(F32)
    return high, middle, rest - middle


def block_transpose(a, b, c, d):
    lane = lanes()
    half = lane < 64
    even = (lane & 32) == 0
    a, c = jnp.where(half, a, pltpu.roll(c, 64, 1)), jnp.where(half, pltpu.roll(a, 64, 1), c)
    b, d = jnp.where(half, b, pltpu.roll(d, 64, 1)), jnp.where(half, pltpu.roll(b, 64, 1), d)
    a, b = jnp.where(even, a, pltpu.roll(b, 32, 1)), jnp.where(even, pltpu.roll(a, 96, 1), b)
    c, d = jnp.where(even, c, pltpu.roll(d, 32, 1)), jnp.where(even, pltpu.roll(c, 96, 1), d)
    return a, b, c, d


def pack(tiles, store, base):
    for first in range(0, len(tiles) // 4, 8):
        rows = [block_transpose(*tiles[4 * k : 4 * k + 4]) for k in range(first, first + 8)]
        for quarter in range(4):
            turned = jnp.swapaxes(jnp.stack([four[quarter] for four in rows]), 0, 1)
            for g in range(8):
                store[quarter * 8 + g, base + first : base + first + 8, :] = turned[g]


def donor_kernel(
    prop_hbm,
    index_hbm,
    fringe_hbm,
    weight_hbm,
    state_hbm,
    thrust_hbm,
    out_ref,
    thrust_out,
    prop_ref,
    index_ref,
    fringe_ref,
    weight_ref,
    state_ref,
    thrust_ref,
    sems,
):
    copies = [
        pltpu.make_async_copy(source, target, sems.at[at])
        for at, (source, target) in enumerate(
            (
                (index_hbm, index_ref),
                (prop_hbm, prop_ref),
                (weight_hbm, weight_ref),
                (fringe_hbm, fringe_ref),
                (state_hbm, state_ref),
                (thrust_hbm, thrust_ref),
            )
        )
    ]
    for copy in copies:
        copy.start()
    place = lax.axis_index("girth")
    for copy in copies[:2]:
        copy.wait()
    index = index_ref[...]
    cells = lax.broadcasted_iota(jnp.int32, (256, 128), 0)
    pick = jnp.where(cells == index, 1.0, 0.0).astype(BF16)
    pad = jnp.zeros((1, 256), F32)
    parts = [jnp.concatenate([part, pad], axis=0) for part in split_parts(prop_ref[...])]
    sums = jnp.dot(jnp.concatenate(parts, axis=0).astype(BF16), pick, preferred_element_type=F32)
    values = (sums[0:8, :] + sums[8:16, :] + sums[16:24, :])[:VARS, :]
    for copy in copies[2:]:
        copy.wait()
    values = values * weight_ref[...]
    target = jnp.where(index >= 0, fringe_ref[...], -1).astype(F32)
    edges = [
        (
            state_ref[pl.ds(row * 56, VARS, stride=8), :],
            state_ref[pl.ds(row * 56 + 7, VARS, stride=8), :],
        )
        for row in range(2)
    ]
    for v in range(VARS):
        thrust_out[v] = jnp.full((8, 128), thrust_ref[v], F32)
    upper = lax.rem(place + 1, GIRTHS)
    for peer in range(GIRTHS):
        start = peer * DONOR_ROWS
        out_ref[start : start + VARS, :] = values
        out_ref[start + VARS : start + 8, :] = target
        out_ref[start + 8 : start + 24, :] = jnp.zeros((16, 128), F32)
        for row, (first, last) in enumerate(edges):
            at = start + 8 + row * 8
            out_ref[at : at + VARS, :] = jnp.where(upper == peer, last, first)


def fringe_sums(landed_ref, place):
    sub, lane = sublanes(), lanes()
    row = lanes((1, 128))
    slot = row & 31
    left = {}
    right = []
    for group in range(4):
        entries = jnp.zeros((8, 128), F32)
        for quarter in range(4):
            sender = group * 4 + quarter
            shift = lax.rem(32 * quarter + 8 - 8 * place + 128, 128)
            rolled = pltpu.roll(landed_ref[sender * DONOR_ROWS : sender * DONOR_ROWS + 8, :], shift, 1)
            entries = jnp.where((lane >> 5) == quarter, rolled, entries)
        target = entries[7:8, :].astype(jnp.int32)
        live = target >= 0
        tall = target >> 7
        own = jnp.where(live & (slot >= 8) & (slot < 16), tall, -1)
        low = jnp.where(live & (slot < 8) & ((tall & 7) == 7), tall >> 3, -1)
        high = jnp.where(live & (slot >= 16) & (slot < 24) & ((tall & 7) == 0), tall >> 3, -1)
        onto = lax.broadcasted_iota(jnp.int32, (128, 128), 0)
        right.append(jnp.where(onto == (target & 127), 1.0, 0.0).astype(BF16))
        parts = split_parts(entries)
        for which, part in enumerate(parts):
            counted = 1.0 if which == 0 else 0.0
            marked = jnp.where(sub == 7, counted, part)
            rows = []
            for r in range(2):
                inside = own == sub + 8 * r
                for v in range(8):
                    rows.append(jnp.where(inside, marked[v : v + 1, :], 0.0))
            for side in (low, high):
                for r in range(2):
                    rows.append(jnp.where(side == r, marked, 0.0))
            left[which, group] = jnp.concatenate(rows, axis=0).astype(BF16)
    right = jnp.concatenate(right, axis=1)
    lhs = jnp.concatenate(
        [
            jnp.concatenate([left[which, group] for group in range(4)], axis=1)
            for which in range(3)
        ],
        axis=0,
    )
    sums = lax.dot_general(lhs, right, (((1,), (1,)), ((), ())), preferred_element_type=F32)
    return sums[0:160, :] + sums[160:320, :] + sums[320:480, :]


def flow_kernel(
    landed_ref,
    state_ref,
    face_ref,
    disk_ref,
    diag_ref,
    thrust_ref,
    coupling_hbm,
    send_ref,
    current_ref,
    down_ref,
    up_ref,
    partial_ref,
    factor_ref,
    coupling_ref,
    sem,
):
    coupling_copy = pltpu.make_async_copy(coupling_hbm, coupling_ref, sem)
    coupling_copy.start()
    tiles = [
        diag_ref[r, i, j].astype(F32) for r in range(2) for i in range(VARS) for j in range(VARS)
    ]
    pack(tiles[2:], send_ref, 8)
    place = lax.axis_index("girth")
    sub, lane = sublanes(), lanes()
    sums = fringe_sums(landed_ref, place)
    edges = []
    for side, peer in enumerate((lax.rem(place + 15, GIRTHS), lax.rem(place + 1, GIRTHS))):
        both = []
        for r in range(2):
            start = pl.multiple_of(peer * DONOR_ROWS + 8 + 8 * r, 8)
            edge = landed_ref[pl.ds(start, 8), :]
            found = sums[128 + side * 16 + r * 8 : 136 + side * 16 + r * 8, :]
            both.append(jnp.where(found[7:8, :] > 0.5, found, edge))
        edges.append(both)
    current, fringe = [], []
    for r in range(2):
        block = sums[r * 64 : (r + 1) * 64, :]
        hit = block[56:64, :] > 0.5
        fringe.append(hit)
        current.append(
            [jnp.where(hit, block[v * 8 : v * 8 + 8, :], state_ref[r, v]) for v in range(VARS)]
        )
    zero = jnp.zeros((8, 128), F32)
    residual = []
    for r in range(2):
        disk = disk_ref[r].astype(F32)
        residual.append([disk * thrust_ref[i] for i in range(VARS)])
    coupling_copy.wait()
    for direction in range(6):
        jumps = []
        for r in range(2):
            own = current[r]
            if direction < 2:
                beside = [zero] * VARS if direction == r else current[1 - r]
            elif direction == 2:
                beside = [
                    jnp.where(sub == 0, edges[0][r][v : v + 1, :], pltpu.roll(own[v], 1, 0))
                    for v in range(VARS)
                ]
            elif direction == 3:
                beside = [
                    jnp.where(sub == 7, edges[1][r][v : v + 1, :], pltpu.roll(own[v], 7, 0))
                    for v in range(VARS)
                ]
            elif direction == 4:
                beside = [jnp.where(lane == 0, 0.0, pltpu.roll(own[v], 1, 1)) for v in range(VARS)]
            else:
                beside = [
                    jnp.where(lane == 127, 0.0, pltpu.roll(own[v], 127, 1)) for v in range(VARS)
                ]
            factor = face_ref[r, direction]
            jumps.append([factor * (beside[v] - own[v]) for v in range(VARS)])
        for i in range(VARS):
            for j in range(VARS):
                weight = coupling_ref[direction, i, j]
                for r in range(2):
                    residual[r][i] = residual[r][i] + weight * jumps[r][j]
    factors = [face_ref[r, r] for r in range(2)]
    passed = []
    for r, ref in enumerate((down_ref, up_ref)):
        passed += [
            total_of([coupling_ref[r, i, j] * current[1 - r][j] for j in range(VARS)])
            for i in range(VARS)
        ]
        factor_ref[r] = factors[r]
        for v in range(VARS):
            ref[v] = passed[r * VARS + v]
            current_ref[r, v] = current[r][v]
            partial_ref[r, v] = residual[r][v]
    flow = [jnp.where(fringe[r], 0.0, x) for r in range(2) for x in residual[r]]
    flow += passed
    flow += [jnp.where(fringe[r], 0.0, factors[r]) for r in range(2)]
    flow += [diag_ref[0, 0, j].astype(F32) for j in range(2)]
    pack(flow, send_ref, 0)


def from_before(x):
    sub, lane = sublanes(), lanes()
    wrapped = jnp.where(lane < 32, 0.0, pltpu.roll(x, 32, 1))
    return jnp.where(sub < 1, pltpu.roll(wrapped, 1, 0), pltpu.roll(x, 1, 0))


def from_after(x):
    sub, lane = sublanes(), lanes()
    wrapped = jnp.where(lane >= 96, 0.0, pltpu.roll(x, 96, 1))
    return jnp.where(sub >= 7, pltpu.roll(wrapped, 7, 0), pltpu.roll(x, 7, 0))


def within_before(x, count, fill=0.0):
    return jnp.where(sublanes() < count, fill, pltpu.roll(x, count, 0))


def within_after(x, count, fill=0.0):
    return jnp.where(sublanes() >= 8 - count, fill, pltpu.roll(x, 8 - count, 0))


def eight_before(x):
    x = jnp.broadcast_to(x[7:8, :], (8, 128))
    return jnp.where(lanes() < 32, 0.0, pltpu.roll(x, 32, 1))


def eight_after(x):
    x = jnp.broadcast_to(x[0:1, :], (8, 128))
    return jnp.where(lanes() >= 96, 0.0, pltpu.roll(x, 96, 1))


def total_of(terms):
    total = terms[0]
    for term in terms[1:]:
        total = total + term
    return total


def apply(ref, vector, add=None):
    result = []
    for i in range(VARS):
        terms = [ref[i * VARS + j] * vector[j] for j in range(VARS)]
        result.append(total_of(terms + ([add[i]] if add is not None else [])))
    return result


def spread_kernel(lower_ref, upper_ref, out_ref):
    for which, ref in enumerate((lower_ref, upper_ref)):
        for i in range(VARS):
            for j in range(VARS):
                out_ref[which, i * VARS + j] = jnp.full((8, 128), ref[i, j], F32)


def solve_kernel(
    moved_ref, spread_ref, back_ref, diag, near, far, maps, moved_maps
):
    flow = []
    for first in range(0, SEND_ROWS, 8):
        tiles = []
        for quarter in range(4):
            loaded = [moved_ref[quarter * 8 + s, first : first + 8, :] for s in range(8)]
            tiles.append(jnp.swapaxes(jnp.stack(loaded), 0, 1))
        for k in range(8):
            for at, tile in enumerate(block_transpose(*[four[k] for four in tiles])):
                place = 4 * (first + k) + at - 30
                if place < 0:
                    flow.append(tile)
                else:
                    diag[place // 49, place % 49] = tile
    beside = [
        [from_before(flow[14 + v]) for v in range(VARS)],
        [from_after(flow[21 + v]) for v in range(VARS)],
    ]
    source = [
        [-flow[r * VARS + i] - flow[28 + r] * beside[r][i] for i in range(VARS)] for r in range(2)
    ]

    def times(which, out):
        for k in range(VARS):
            column = [spread_ref[which, j * VARS + k] for j in range(VARS)]
            for r in range(2):
                for i in range(VARS):
                    out[r, i * VARS + k] = total_of(
                        [diag[r, i * VARS + j] * column[j] for j in range(VARS)]
                    )

    def multiply(a, b, out):
        for i in range(VARS):
            row = [a[i * VARS + j] for j in range(VARS)]
            for k in range(VARS):
                out[i * VARS + k] = total_of([row[j] * b[j * VARS + k] for j in range(VARS)])

    def scan(offset, within, eight):
        for level, count in enumerate((1, 2, 4)):
            a = maps.at[level]
            for at in range(49):
                moved_maps[at] = within(a[at], count, float(at // VARS == at % VARS))
            offset = apply(a, [within(x, count) for x in offset], offset)
            multiply(a, moved_maps, maps.at[level + 1])
        a = maps.at[3]
        x = offset
        for _ in range(3):
            x = apply(a, [eight(part) for part in x], offset)
        return x

    times(0, near)
    times(1, far)
    first = apply(diag.at[0], source[0])
    second = apply(near.at[1], first, apply(diag.at[1], source[1]))
    multiply(near.at[1], near.at[0], maps.at[0])
    second = scan(second, within_before, eight_before)
    first = apply(near.at[0], [from_before(x) for x in second], first)
    multiply(far.at[0], far.at[1], maps.at[0])
    update_first = scan(apply(far.at[0], second, first), within_after, eight_after)
    update_second = apply(far.at[1], [from_after(x) for x in update_first], second)

    results = update_first + update_second + [jnp.zeros((8, 128), F32)] * 2
    for k in range(BACK_ROWS):
        for quarter, tile in enumerate(block_transpose(*results[4 * k : 4 * k + 4])):
            back_ref[pl.ds(quarter * 8 * BACK_ROWS + k, 8, stride=BACK_ROWS), :] = tile


def finish_kernel(
    returned_ref, current_ref, partial_ref, factor_ref, low_ref, high_ref, state_ref, residual_ref
):
    results = []
    for k in range(BACK_ROWS):
        results += block_transpose(
            *[
                returned_ref[pl.ds(quarter * 8 * BACK_ROWS + k, 8, stride=BACK_ROWS), :]
                for quarter in range(4)
            ]
        )
    for r, ref in enumerate((low_ref, high_ref)):
        for v in range(VARS):
            state_ref[r, v] = current_ref[r, v] + results[r * VARS + v]
            residual_ref[r, v] = partial_ref[r, v] + factor_ref[r] * ref[v]


VMEM = pl.BlockSpec(memory_space=pltpu.VMEM)
SMEM = pl.BlockSpec(memory_space=pltpu.SMEM)
HBM = pl.BlockSpec(memory_space=pltpu.HBM)


def exchange(block, axis, parts):
    rows = block.shape[0] // parts
    shaped = block.reshape(parts, rows, 128)
    return lax.all_to_all(shaped, axis, 0, 0, tiled=True).reshape(block.shape)


def per_device(
    state,
    propeller,
    donor_index,
    fringe_index,
    donor_weight,
    disk_mask,
    thrust,
    face,
    coupling,
    diag_inverse,
    lower_jacobian,
    upper_jacobian,
):
    inputs = (propeller, donor_index, fringe_index, donor_weight, state.reshape(112, 128), thrust)
    inputs = [pltpu.with_memory_space_constraint(x, pltpu.HBM) for x in inputs]
    donors, thrusts = pl.pallas_call(
        donor_kernel,
        out_shape=(
            jax.ShapeDtypeStruct((GIRTHS * DONOR_ROWS, 128), F32),
            jax.ShapeDtypeStruct((VARS, 8, 128), F32),
        ),
        in_specs=[HBM] * 6,
        out_specs=(VMEM, VMEM),
        scratch_shapes=[
            pltpu.VMEM((VARS, 256), F32),
            pltpu.VMEM((1, 128), jnp.int32),
            pltpu.VMEM((1, 128), jnp.int32),
            pltpu.VMEM((1, 128), F32),
            pltpu.VMEM((112, 128), F32),
            pltpu.SMEM((VARS,), F32),
            pltpu.SemaphoreType.DMA((6,)),
        ],
        compiler_params=pltpu.CompilerParams(vmem_limit_bytes=4 << 20),
        name="donors",
    )(*inputs)
    landed = exchange(donors, "girth", GIRTHS)
    row = jax.ShapeDtypeStruct(state.shape[1:], F32)
    both = jax.ShapeDtypeStruct(state.shape, F32)
    send, current, down, up, partial, factor = pl.pallas_call(
        flow_kernel,
        out_shape=(
            jax.ShapeDtypeStruct((STREAMS, SEND_ROWS, 128), F32),
            both,
            row,
            row,
            both,
            jax.ShapeDtypeStruct((2, 8, 128), F32),
        ),
        in_specs=[VMEM] * 6 + [pl.BlockSpec(memory_space=pl.ANY)],
        out_specs=(VMEM,) * 6,
        scratch_shapes=[pltpu.SMEM((6, VARS, VARS), F32), pltpu.SemaphoreType.DMA(())],
        compiler_params=pltpu.CompilerParams(vmem_limit_bytes=16 << 20),
        name="flow",
    )(landed, state, face, disk_mask, diag_inverse, thrusts, coupling)
    moved = lax.all_to_all(send, "stream", 0, 0, tiled=True)
    ahead = [(at, at + 1) for at in range(STREAMS - 1)]
    low = lax.ppermute(down, "stream", ahead)
    high = lax.ppermute(up, "stream", [(b, a) for a, b in ahead])
    lower, upper, _ = lax.optimization_barrier((lower_jacobian, upper_jacobian, factor))
    spread = pl.pallas_call(
        spread_kernel,
        out_shape=jax.ShapeDtypeStruct((2, VARS * VARS, 8, 128), F32),
        in_specs=[SMEM] * 2,
        out_specs=VMEM,
        compiler_params=pltpu.CompilerParams(vmem_limit_bytes=4 << 20),
        name="spread",
    )(lower, upper)
    back = pl.pallas_call(
        solve_kernel,
        out_shape=jax.ShapeDtypeStruct((STREAMS * BACK_ROWS, 128), F32),
        in_specs=[VMEM] * 2,
        out_specs=VMEM,
        scratch_shapes=[
            pltpu.VMEM((2, 49, 8, 128), F32),
            pltpu.VMEM((2, 49, 8, 128), F32),
            pltpu.VMEM((2, 49, 8, 128), F32),
            pltpu.VMEM((4, 49, 8, 128), F32),
            pltpu.VMEM((49, 8, 128), F32),
        ],
        compiler_params=pltpu.CompilerParams(vmem_limit_bytes=16 << 20),
        name="solve",
    )(moved, spread)
    back, low, high = lax.optimization_barrier((back, low, high))
    returned = exchange(back, "stream", STREAMS)
    return pl.pallas_call(
        finish_kernel,
        out_shape=(both, both),
        in_specs=[VMEM] * 6,
        out_specs=(VMEM, VMEM),
        compiler_params=pltpu.CompilerParams(vmem_limit_bytes=4 << 20),
        name="finish",
    )(returned, current, partial, factor, low, high)


def solution(mesh):
    placed = (
        P("stream", None, "girth", None),
        P(None, ("stream", "girth")),
        P(("stream", "girth"), None),
        P(("stream", "girth"), None),
        P(("stream", "girth"), None),
        P("stream", "girth", None),
        P(),
        P("stream", None, "girth", None),
        P(),
        P("stream", None, None, "girth", None),
        P(),
        P(),
    )
    return jax.shard_map(
        per_device,
        mesh=mesh,
        in_specs=placed,
        out_specs=(P("stream", None, "girth", None), P("stream", None, "girth", None)),
        check_vma=False,
    )
```
